128 devices in a mesh: dp: 16 (over x, y_lo, core), ctx: 8 (over y_hi, z).
Axes of the slice: x: 4, y: 4 (y_hi: 2, y_lo: 2; y = y_hi * 2 + y_lo), z: 4, core: 2. Of those that a mesh axis runs over, the one named last changes fastest.
Arguments:
- tokens: bfloat16 [16, 1792, 2048], P('dp', 'ctx'), may hold values from -6 to 6
- norm_gain: bfloat16 [2048], replicated, may hold values from 0.099609375 to 1.8984375
- q_weight: bfloat16 [2048, 2048], P('dp'), may hold values from -0.110927376 to 0.110927376
- k_weight: bfloat16 [2048, 2048], P('dp'), may hold values from -6.408155204503087 to 6.408155204503087
- v_weight: bfloat16 [2048, 2048], P('dp'), may hold values from -0.125 to 0.125
Outputs:
- attended: bfloat16 [16, 1792, 2048], P('dp', 'ctx')
The draws below stay inside these ranges and needn't reach their ends.
All inputs are finite; a program needn't handle non-finite values.
Results may differ from the reference program's by a relative error of at most 0.0055.
The reference program's roundings to bfloat16 on the way (of `normed`, `values` and `probs`) count: a program that leaves them out, or rounds other values in their place, can miss the bound.
Values may be sent and summed in bfloat16 or wider, within the bound.
A program may use at most 128 MiB of HBM per device.

```python
import jax
import jax.numpy as jnp
from jax import lax

D = 2048
HEADS = 16
HEAD_DIM = 128
SEQS = 16
LEN = 1792


def weight_pair(key):
    columns = HEADS * HEAD_DIM
    query = jnp.clip(jax.random.normal(jax.random.fold_in(key, 11), (D, columns), jnp.float32), -5.0, 5.0) * D ** (-0.5)
    other = jnp.clip(jax.random.normal(jax.random.fold_in(key, 12), (D, columns), jnp.float32), -5.0, 5.0) * D ** (-0.5)
    return (query, other)


def draw_q_weight(key, part):
    return weight_pair(key)[0].astype(jnp.bfloat16)


def draw_k_weight(key, part):
    return weight_pair(key)[1].astype(jnp.bfloat16)


def draw_tokens(key, part):
    base = jnp.clip(jax.random.normal(jax.random.fold_in(key, 21), (SEQS, LEN, D), jnp.float32), -6.0, 6.0)
    return base.astype(jnp.bfloat16)


def level_of(stream_key, shape, split, smallest, high):
    level = 1.0
    for position, parts in split:
        heights = jax.random.uniform(jax.random.fold_in(jax.random.fold_in(stream_key, 6), position), (parts,), jnp.float32, smallest / len(split), high / len(split))
        level = level * jnp.repeat(jnp.exp(heights), shape[position] // parts).reshape((-1,) + (1,) * (len(shape) - 1 - position))
    return level


def normal_values(key, shape, width, reach, shards=(), kind=jnp.bfloat16):
    result = width * jax.random.normal(key, shape, jnp.float32)
    if shards:
        result = result * level_of(key, shape, shards, -0.22, 0.18)
    return jnp.clip(result, -reach, reach).astype(kind)


def setup_inputs(seed: int = 0) -> dict:
    key_list = jax.random.split(jax.random.key(seed), 6)
    return {
        "tokens": draw_tokens(jax.random.fold_in(key_list[5], 71), 0),
        "norm_gain": jnp.clip(1.0 + 0.18 * jax.random.normal(key_list[1], (D,), jnp.float32), 0.099609375, 1.8984375).astype(jnp.bfloat16),
        "q_weight": draw_q_weight(jax.random.fold_in(key_list[5], 71), 0),
        "k_weight": draw_k_weight(jax.random.fold_in(key_list[5], 71), 0),
        "v_weight": normal_values(key_list[4], (D, HEADS * HEAD_DIM), D ** -0.5, 0.125, ((0, 16),)),
    }


def rotate(values, positions):
    half = HEAD_DIM // 2
    shaped = values.reshape(values.shape[0], HEADS, HEAD_DIM)
    freqs = 10000.0 ** (-(jnp.arange(half).astype(jnp.float32) * 2.0) / HEAD_DIM)
    angles = positions[:, None] * freqs[None, :]
    cosine = jnp.cos(angles)[:, None, :]
    sine = jnp.sin(angles)[:, None, :]
    first = shaped[:, :, :half]
    second = shaped[:, :, half:]
    turned = jnp.concatenate([first * cosine - second * sine, second * cosine + first * sine], axis=2)
    return turned.reshape(values.shape[0], HEADS * HEAD_DIM)

def one_sequence(sequence, norm_gain, q_weight, k_weight, v_weight):
    rows = sequence.astype(jnp.float32)
    scale_rows = lax.rsqrt(lax.optimization_barrier(jnp.mean(rows * rows, axis=1, keepdims=True)) + 1e-05)
    normed = (rows * scale_rows * norm_gain.astype(jnp.float32)[None, :]).astype(jnp.bfloat16)
    q_lin = jnp.dot(normed, q_weight, preferred_element_type=jnp.float32)
    k_lin = jnp.dot(normed, k_weight, preferred_element_type=jnp.float32)
    v_lin = jnp.dot(normed, v_weight, preferred_element_type=jnp.float32)
    values = v_lin.astype(jnp.bfloat16)
    positions = jnp.arange(LEN).astype(jnp.float32)
    queries = rotate(q_lin, positions).astype(jnp.bfloat16)
    keys = rotate(k_lin, positions).astype(jnp.bfloat16)
    head_q = queries.reshape(LEN, HEADS, HEAD_DIM).transpose(1, 0, 2)
    head_k = keys.reshape(LEN, HEADS, HEAD_DIM).transpose(1, 0, 2)
    head_v = values.reshape(LEN, HEADS, HEAD_DIM).transpose(1, 0, 2)
    allowed = jnp.arange(LEN)[None, :] <= jnp.arange(LEN)[:, None]
    factor = HEAD_DIM ** (-0.5)

    def one_head(triple):
        qa, ka, va = triple
        scores = jnp.dot(qa, ka.T, preferred_element_type=jnp.float32) * factor
        scores = jnp.where(allowed, scores, -1e+30)
        top = lax.optimization_barrier(jnp.max(scores, axis=1, keepdims=True))
        expo = jnp.where(allowed, jnp.exp(scores - top), 0.0)
        probs = expo.astype(jnp.bfloat16)
        numer = jnp.dot(probs, va, preferred_element_type=jnp.float32)
        return numer / lax.optimization_barrier(jnp.sum(expo, axis=1, keepdims=True))
    outputs = lax.map(one_head, (head_q, head_k, head_v))
    return outputs.transpose(1, 0, 2).reshape(LEN, HEADS * HEAD_DIM).astype(jnp.bfloat16)

def reference(tokens, norm_gain, q_weight, k_weight, v_weight):
    return lax.map(lambda sequence: one_sequence(sequence, norm_gain, q_weight, k_weight, v_weight), tokens)
```

```python
import functools
import math

import jax
import jax.numpy as jnp
import numpy as np
from jax import lax
from jax.experimental import pallas as pl
from jax.experimental.pallas import tpu as pltpu
from jax.sharding import PartitionSpec as P

MESH = pl.DeviceIdType.MESH
HEADS = 16
HD = 128
D = 2048
ROWS = 224
LEN = 1792
WR = 128
WC = 256
HALF = ROWS // 2
QB = 256
NQ = LEN // QB
NCHUNK = 32
PB = 448


def tables():
    freqs = 10000.0 ** (-2.0 * np.arange(HD // 2) / HD)
    angles = np.arange(LEN)[:, None] * freqs[None, :]
    cosine, sine = np.cos(angles), np.sin(angles)
    return (
        np.concatenate([cosine, cosine], axis=1).astype(np.float32),
        np.concatenate([-sine, sine], axis=1).astype(np.float32),
    )


def kernel(
    tok, gain, qw, kw, vw, cos_hbm, sin_hbm, out,
    tbuf, nbuf, wbuf, qbuf, kbuf, vbuf, obuf, cosb, sinb,
    wrecv, wsend, trecv, tsend, precv, psend, osend, orecv, lsem,
):
    d, t = lax.axis_index("dp"), lax.axis_index("ctx")
    x, yl, c = d // 4, (d // 2) % 2, d % 2
    yh, z = t // 4, t % 4
    y = yh * 2 + yl
    home = c == yh
    away = c != yh

    def dev(x_, yl_, c_, yh_, z_):
        return (x_ * 4 + yl_ * 2 + c_, yh_ * 4 + z_)

    def chip_y(step, c_):
        y_ = (y + step) % 4
        return dev(x, y_ % 2, c_, y_ // 2, z)

    partner = dev(x, yl, 1 - c, yh, z)
    pair = dev(x, yl, 1 - c, 1 - yh, z)
    xp, xm = dev((x + 1) % 4, yl, c, yh, z), dev((x + 3) % 4, yl, c, yh, z)
    zp, zm = dev(x, yl, c, yh, (z + 1) % 4), dev(x, yl, c, yh, (z + 3) % 4)

    def send(src, dst, ss, rs, to):
        return pltpu.make_async_remote_copy(
            src_ref=src, dst_ref=dst, send_sem=ss, recv_sem=rs, device_id=to, device_id_type=MESH
        )

    def wslot(e):
        return wbuf.at[:, pl.ds(pl.multiple_of(e * WR, WR), WR), :]

    def wslot_one(i, e):
        return wbuf.at[i, pl.ds(pl.multiple_of(e * WR, WR), WR), :]

    def wcols(ref, c_):
        return ref.at[:, pl.ds(pl.multiple_of(z * 512 + c_ * WC, WC), WC)]

    def tslot(z_, h):
        return tbuf.at[c * 4 + z_, pl.ds(h * HALF, HALF), :]

    weights = (qw, kw, vw)
    for i, w in enumerate(weights):
        pltpu.make_async_copy(wcols(w, c), wslot_one(i, d), wrecv.at[0, 0]).start()

    @pl.when(home)
    def _():
        for h in range(2):
            pltpu.make_async_copy(tok.at[pl.ds(h * HALF, HALF), :], tslot(z, h), trecv.at[0, h]).start()

    pltpu.make_async_copy(cos_hbm, cosb, lsem.at[0]).start()
    pltpu.make_async_copy(sin_hbm, sinb, lsem.at[1]).start()

    barrier = pltpu.get_barrier_semaphore()

    def greet(to):
        pl.semaphore_signal(barrier, inc=1, device_id=to, device_id_type=MESH)

    for k in range(1, 16):
        j = (c * 8 + t + k) % 16
        greet((x * 4 + yl * 2 + j // 8, j % 8))
    greet(xp)
    greet(xm)
    for step in (1, 3):
        for c_ in range(2):
            greet(chip_y(step, c_))
    pl.semaphore_wait(barrier, 21)

    for i, w in enumerate(weights):
        send(wcols(w, c), wslot_one(i, d), wsend.at[0, 0], wrecv.at[0, 2], chip_y(1, c)).start()
        send(wcols(w, 1 - c), wslot_one(i, d), wsend.at[0, 1], wrecv.at[0, 3], chip_y(3, 1 - c)).start()
        send(wcols(w, 1 - c), wslot_one(i, d), wsend.at[0, 2], wrecv.at[0, 1], partner).start()

    def exchange(h):
        there = tbuf.at[(1 - c) * 4 + z, pl.ds(h * HALF, HALF), :]
        return send(tok.at[pl.ds(h * HALF, HALF), :], there, tsend.at[0, h], trecv.at[0, h], pair)

    @pl.when(away)
    def _():
        exchange(0).start()
        exchange(1).start()

    own = [d, x * 4 + yl * 2 + (1 - c), x * 4 + (1 - yl) * 2 + c, x * 4 + (1 - yl) * 2 + (1 - c)]

    def shift(e, s):
        return (e + 4 * s) % 16

    def wait_w(g, k, e):
        send(wslot(e), wslot(e), wsend.at[0, 0], wrecv.at[g, k], partner).wait_recv()

    def wait_w_local():
        for i, w in enumerate(weights):
            pltpu.make_async_copy(wcols(w, c), wslot_one(i, d), wrecv.at[0, 0]).wait()

    def x_first(k):
        e = own[k]
        return (
            send(wslot(e), wslot(e), wsend.at[1, k], wrecv.at[1, k], xp),
            send(wslot(e), wslot(e), wsend.at[2, k], wrecv.at[2, k], xm),
        )

    def x_second(k):
        if k % 2 == 0:
            e = shift(own[k], 3)
            return send(wslot(e), wslot(e), wsend.at[3, k], wrecv.at[3, k], xp)
        e = shift(own[k], 1)
        return send(wslot(e), wslot(e), wsend.at[3, k], wrecv.at[3, k], xm)

    def z_first(h):
        return (
            send(tslot(z, h), tslot(z, h), tsend.at[1, h], trecv.at[1, h], zp),
            send(tslot(z, h), tslot(z, h), tsend.at[2, h], trecv.at[2, h], zm),
        )

    def z_second(h):
        z_ = (z + (3, 1)[h]) % 4
        return send(tslot(z_, h), tslot(z_, h), tsend.at[3, h], trecv.at[3, h], (zp, zm)[h])

    zs = [z, (z + 3) % 4, (z + 1) % 4, (z + 2) % 4]

    def to_partner(g, h):
        return send(tslot(zs[g], h), tslot(zs[g], h), psend.at[g, h], precv.at[g, h], partner)

    def wait_t(g, h):
        send(tslot(zs[g], h), tslot(zs[g], h), tsend.at[1, h], trecv.at[g, h], partner).wait_recv()

    def wait_own_t(h):
        @pl.when(home)
        def _():
            pltpu.make_async_copy(tok.at[pl.ds(h * HALF, HALF), :], tslot(z, h), trecv.at[0, h]).wait()

        @pl.when(away)
        def _():
            wait_t(0, h)

    def start_both(pair_):
        pair_[0].start()
        pair_[1].start()

    wait_w_local()
    start_both(x_first(0))

    @pl.when(home)
    def _():
        for h in range(2):
            wait_own_t(h)
            start_both(z_first(h))
            to_partner(0, h).start()

    for k in range(1, 4):
        wait_w(0, k, own[k])
        start_both(x_first(k))

    @pl.when(away)
    def _():
        for h in range(2):
            wait_own_t(h)
            start_both(z_first(h))
            to_partner(0, h).start()

    wait_w(1, 0, shift(own[0], 3))
    x_second(0).start()
    wait_w(2, 1, shift(own[1], 1))
    x_second(1).start()
    wait_t(1, 0)
    z_second(0).start()
    to_partner(1, 0).start()
    wait_t(2, 1)
    z_second(1).start()
    to_partner(2, 1).start()
    wait_w(1, 2, shift(own[2], 3))
    x_second(2).start()
    wait_w(2, 3, shift(own[3], 1))
    x_second(3).start()
    wait_t(1, 1)
    to_partner(1, 1).start()
    wait_t(2, 0)
    to_partner(2, 0).start()
    wait_t(3, 0)
    to_partner(3, 0).start()
    wait_t(3, 1)
    to_partner(3, 1).start()
    for k in (1, 3):
        wait_w(1, k, shift(own[k], 3))
    for k in (0, 2):
        wait_w(2, k, shift(own[k], 1))
    for k in range(4):
        wait_w(3, k, shift(own[k], 2))

    def pslot(z_, h):
        return tbuf.at[(1 - c) * 4 + z_, pl.ds(h * HALF, HALF), :]

    for g in range(4):
        for h in range(2):
            send(pslot(zs[g], h), pslot(zs[g], h), psend.at[g, h], precv.at[g, h], partner).wait_recv()
    pltpu.make_async_copy(cos_hbm, cosb, lsem.at[0]).wait()
    pltpu.make_async_copy(sin_hbm, sinb, lsem.at[1]).wait()

    gain_row = gain[...].astype(jnp.float32)

    def norm_rows(i, carry):
        block, part = i // (ROWS // NCHUNK), i % (ROWS // NCHUNK)
        rows = tbuf[block, pl.ds(pl.multiple_of(part * NCHUNK, NCHUNK), NCHUNK), :].astype(jnp.float32)
        scale = lax.rsqrt(jnp.mean(rows * rows, axis=1, keepdims=True) + 1e-05)
        nbuf[pl.ds(pl.multiple_of(i * NCHUNK, NCHUNK), NCHUNK), :] = (rows * scale * gain_row).astype(jnp.bfloat16)
        return carry

    lax.fori_loop(0, LEN // NCHUNK, norm_rows, 0)

    def turned(lin, rows):
        cosine, sine = cosb[rows, :], sinb[rows, :]
        parts = []
        for h in range(2):
            v = lin[:, h * HD : (h + 1) * HD]
            parts.append((v * cosine + pltpu.roll(v, HD // 2, 1) * sine).astype(jnp.bfloat16))
        return parts

    def project(i, carry):
        rows = pl.ds(pl.multiple_of(i * PB, PB), PB)
        block = nbuf[rows, :]
        q = jnp.dot(block, wbuf[0], preferred_element_type=jnp.float32)
        for h, part in enumerate(turned(q, rows)):
            qbuf[h, rows, :] = part
        k = jnp.dot(block, wbuf[1], preferred_element_type=jnp.float32)
        for h, part in enumerate(turned(k, rows)):
            kbuf[h, rows, :] = part
        v = jnp.dot(block, wbuf[2], preferred_element_type=jnp.float32).astype(jnp.bfloat16)
        for h in range(2):
            vbuf[h, rows, :] = v[:, h * HD : (h + 1) * HD]
        return carry

    lax.fori_loop(0, LEN // PB, project, 0)

    factor = HD ** (-0.5) * math.log2(math.e)
    nt = (((1,), (1,)), ((), ()))
    rows_i = lax.broadcasted_iota(jnp.int32, (QB, QB), 0)
    cols_i = lax.broadcasted_iota(jnp.int32, (QB, QB), 1)
    allowed = cols_i <= rows_i
    mycols = pl.ds(pl.multiple_of(z * 512 + c * WC, WC), WC)

    def to_owner(b):
        return send(
            obuf.at[pl.ds(b * ROWS, ROWS), :], out.at[:, mycols], osend.at[b], orecv.at[z * 2 + c],
            dev(x, yl, yh, b // 4, b % 4),
        )

    def to_self(b):
        return pltpu.make_async_copy(obuf.at[pl.ds(b * ROWS, ROWS), :], out.at[:, mycols], osend.at[b])

    def own_block(b):
        return jnp.logical_and(home, t == b)

    sent = 0
    for j in range(NQ):

        def one_head(h, carry, j=j):
            q = qbuf[h, pl.ds(j * QB, QB), :]
            s_d = lax.dot_general(q, kbuf[h, pl.ds(j * QB, QB), :], nt, preferred_element_type=jnp.float32)
            s_d = jnp.where(allowed, s_d, -1e30)
            top = jnp.max(s_d, axis=1, keepdims=True)
            if j:
                s_p = lax.dot_general(q, kbuf[h, pl.ds(0, j * QB), :], nt, preferred_element_type=jnp.float32)
                top = jnp.maximum(top, jnp.max(s_p, axis=1, keepdims=True))
            e_d = jnp.exp2((s_d - top) * factor)
            total = jnp.sum(e_d, axis=1, keepdims=True)
            acc = jnp.dot(e_d.astype(jnp.bfloat16), vbuf[h, pl.ds(j * QB, QB), :], preferred_element_type=jnp.float32)
            if j:
                e_p = jnp.exp2((s_p - top) * factor)
                total = total + jnp.sum(e_p, axis=1, keepdims=True)
                acc = acc + jnp.dot(
                    e_p.astype(jnp.bfloat16), vbuf[h, pl.ds(0, j * QB), :], preferred_element_type=jnp.float32
                )
            obuf[pl.ds(j * QB, QB), pl.ds(pl.multiple_of(h * HD, HD), HD)] = (acc / total).astype(jnp.bfloat16)
            return carry

        lax.fori_loop(0, 2, one_head, 0)
        while sent < 8 and (sent + 1) * ROWS <= (j + 1) * QB:

            @pl.when(own_block(sent))
            def _(b=sent):
                to_self(b).start()

            @pl.when(jnp.logical_not(own_block(sent)))
            def _(b=sent):
                to_owner(b).start()

            sent += 1

    for z_ in range(4):
        for c_ in range(2):
            cols = pl.ds((z_ * 2 + c_) * WC, WC)
            mine = jnp.logical_and(home, jnp.logical_and(z == z_, c == c_))

            @pl.when(jnp.logical_not(mine))
            def _(i=z_ * 2 + c_, cols=cols):
                send(obuf.at[pl.ds(0, ROWS), :], out.at[:, cols], osend.at[0], orecv.at[i], partner).wait_recv()

    for b in range(8):

        @pl.when(own_block(b))
        def _(b=b):
            to_self(b).wait()

        @pl.when(jnp.logical_not(own_block(b)))
        def _(b=b):
            to_owner(b).wait_send()

    for i in range(3):
        send(wslot(d), wslot(d), wsend.at[0, i], wrecv.at[0, 0], partner).wait_send()
    for k in range(4):
        for copy in x_first(k):
            copy.wait_send()
        x_second(k).wait_send()
    for h in range(2):

        @pl.when(away)
        def _(h=h):
            exchange(h).wait_send()

        for copy in z_first(h):
            copy.wait_send()
        z_second(h).wait_send()
        for g in range(4):
            to_partner(g, h).wait_send()


def shards(tokens, norm_gain, q_weight, k_weight, v_weight):
    cosine, sine = tables()
    anywhere = pl.BlockSpec(memory_space=pl.ANY)
    bf, dma = jnp.bfloat16, pltpu.SemaphoreType.DMA
    attended = pl.pallas_call(
        kernel,
        out_shape=jax.ShapeDtypeStruct((ROWS, D), bf),
        in_specs=[anywhere, pl.BlockSpec(memory_space=pltpu.VMEM)] + [anywhere] * 5,
        out_specs=anywhere,
        scratch_shapes=[
            pltpu.VMEM((8, ROWS, D), bf),
            pltpu.VMEM((LEN, D), bf),
            pltpu.VMEM((3, D, WC), bf),
            pltpu.VMEM((2, LEN, HD), bf),
            pltpu.VMEM((2, LEN, HD), bf),
            pltpu.VMEM((2, LEN, HD), bf),
            pltpu.VMEM((LEN, WC), bf),
            pltpu.VMEM((LEN, HD), jnp.float32),
            pltpu.VMEM((LEN, HD), jnp.float32),
            dma((4, 4)),
            dma((4, 4)),
            dma((4, 2)),
            dma((4, 2)),
            dma((4, 2)),
            dma((4, 2)),
            dma((8,)),
            dma((8,)),
            dma((2,)),
        ],
        compiler_params=pltpu.CompilerParams(
            collective_id=0, has_side_effects=True, vmem_limit_bytes=60 * 2**20
        ),
        name="attention_block",
    )(tokens[0], norm_gain[None, :], q_weight, k_weight, v_weight, jnp.asarray(cosine), jnp.asarray(sine))
    return attended[None]


def solution(mesh):
    placed = (P("dp", "ctx", None), P(), P("dp", None), P("dp", None), P("dp", None))
    return jax.shard_map(
        shards, mesh=mesh, in_specs=placed, out_specs=P("dp", "ctx", None), check_vma=False
    )
```

```python
import functools
import math

import jax
import jax.numpy as jnp
import numpy as np
from jax import lax
from jax.experimental import pallas as pl
from jax.experimental.pallas import tpu as pltpu
from jax.sharding import PartitionSpec as P

MESH = pl.DeviceIdType.MESH
HEADS = 16
HD = 128
D = 2048
ROWS = 224
LEN = 1792
WR = 128
WC = 256
HALF = ROWS // 2
QB = 256
NQ = LEN // QB
NCHUNK = 32


def tables():
    freqs = 10000.0 ** (-2.0 * np.arange(HD // 2) / HD)
    angles = np.arange(LEN)[:, None] * freqs[None, :]
    cosine, sine = np.cos(angles), np.sin(angles)
    return (
        np.concatenate([cosine, cosine], axis=1).astype(np.float32),
        np.concatenate([-sine, sine], axis=1).astype(np.float32),
    )


def kernel(
    tok, gain, qw, kw, vw, cos_hbm, sin_hbm, out,
    tbuf, nbuf, wbuf, qbuf, kbuf, vbuf, obuf, cosb, sinb,
    wrecv, wsend, trecv, tsend, precv, psend, osend, orecv, lsem,
):
    d, t = lax.axis_index("dp"), lax.axis_index("ctx")
    x, yl, c = d // 4, (d // 2) % 2, d % 2
    yh, z = t // 4, t % 4
    y = yh * 2 + yl
    home = c == yh
    away = c != yh

    def dev(x_, yl_, c_, yh_, z_):
        return (x_ * 4 + yl_ * 2 + c_, yh_ * 4 + z_)

    def chip_y(step, c_):
        y_ = (y + step) % 4
        return dev(x, y_ % 2, c_, y_ // 2, z)

    partner = dev(x, yl, 1 - c, yh, z)
    pair = dev(x, yl, 1 - c, 1 - yh, z)
    xp, xm = dev((x + 1) % 4, yl, c, yh, z), dev((x + 3) % 4, yl, c, yh, z)
    zp, zm = dev(x, yl, c, yh, (z + 1) % 4), dev(x, yl, c, yh, (z + 3) % 4)

    def send(src, dst, ss, rs, to):
        return pltpu.make_async_remote_copy(
            src_ref=src, dst_ref=dst, send_sem=ss, recv_sem=rs, device_id=to, device_id_type=MESH
        )

    def wslot(e):
        return wbuf.at[:, pl.ds(pl.multiple_of(e * WR, WR), WR), :]

    def wslot_one(i, e):
        return wbuf.at[i, pl.ds(pl.multiple_of(e * WR, WR), WR), :]

    def wcols(ref, c_):
        return ref.at[:, pl.ds(pl.multiple_of(z * 512 + c_ * WC, WC), WC)]

    def tslot(z_, h):
        return tbuf.at[c * 4 + z_, pl.ds(h * HALF, HALF), :]

    weights = (qw, kw, vw)
    for i, w in enumerate(weights):
        pltpu.make_async_copy(wcols(w, c), wslot_one(i, d), wrecv.at[0, 0]).start()

    @pl.when(home)
    def _():
        for h in range(2):
            pltpu.make_async_copy(tok.at[pl.ds(h * HALF, HALF), :], tslot(z, h), trecv.at[0, h]).start()

    pltpu.make_async_copy(cos_hbm, cosb, lsem.at[0]).start()
    pltpu.make_async_copy(sin_hbm, sinb, lsem.at[1]).start()

    barrier = pltpu.get_barrier_semaphore()

    def greet(to):
        pl.semaphore_signal(barrier, inc=1, device_id=to, device_id_type=MESH)

    for k in range(1, 16):
        j = (c * 8 + t + k) % 16
        greet((x * 4 + yl * 2 + j // 8, j % 8))
    greet(xp)
    greet(xm)
    for step in (1, 3):
        for c_ in range(2):
            greet(chip_y(step, c_))
    pl.semaphore_wait(barrier, 21)

    for i, w in enumerate(weights):
        send(wcols(w, c), wslot_one(i, d), wsend.at[0, 0], wrecv.at[0, 2], chip_y(1, c)).start()
        send(wcols(w, 1 - c), wslot_one(i, d), wsend.at[0, 1], wrecv.at[0, 3], chip_y(3, 1 - c)).start()
        send(wcols(w, 1 - c), wslot_one(i, d), wsend.at[0, 2], wrecv.at[0, 1], partner).start()

    def exchange(h):
        there = tbuf.at[(1 - c) * 4 + z, pl.ds(h * HALF, HALF), :]
        return send(tok.at[pl.ds(h * HALF, HALF), :], there, tsend.at[0, h], trecv.at[0, h], pair)

    @pl.when(away)
    def _():
        exchange(0).start()
        exchange(1).start()

    own = [d, x * 4 + yl * 2 + (1 - c), x * 4 + (1 - yl) * 2 + c, x * 4 + (1 - yl) * 2 + (1 - c)]

    def shift(e, s):
        return (e + 4 * s) % 16

    def wait_w(g, k, e):
        send(wslot(e), wslot(e), wsend.at[0, 0], wrecv.at[g, k], partner).wait_recv()

    def wait_w_local():
        for i, w in enumerate(weights):
            pltpu.make_async_copy(wcols(w, c), wslot_one(i, d), wrecv.at[0, 0]).wait()

    def x_first(k):
        e = own[k]
        return (
            send(wslot(e), wslot(e), wsend.at[1, k], wrecv.at[1, k], xp),
            send(wslot(e), wslot(e), wsend.at[2, k], wrecv.at[2, k], xm),
        )

    def x_second(k):
        if k % 2 == 0:
            e = shift(own[k], 3)
            return send(wslot(e), wslot(e), wsend.at[3, k], wrecv.at[3, k], xp)
        e = shift(own[k], 1)
        return send(wslot(e), wslot(e), wsend.at[3, k], wrecv.at[3, k], xm)

    def z_first(h):
        return (
            send(tslot(z, h), tslot(z, h), tsend.at[1, h], trecv.at[1, h], zp),
            send(tslot(z, h), tslot(z, h), tsend.at[2, h], trecv.at[2, h], zm),
        )

    def z_second(h):
        z_ = (z + (3, 1)[h]) % 4
        return send(tslot(z_, h), tslot(z_, h), tsend.at[3, h], trecv.at[3, h], (zp, zm)[h])

    zs = [z, (z + 3) % 4, (z + 1) % 4, (z + 2) % 4]

    def to_partner(g, h):
        return send(tslot(zs[g], h), tslot(zs[g], h), psend.at[g, h], precv.at[g, h], partner)

    def wait_t(g, h):
        send(tslot(zs[g], h), tslot(zs[g], h), tsend.at[1, h], trecv.at[g, h], partner).wait_recv()

    def wait_own_t(h):
        @pl.when(home)
        def _():
            pltpu.make_async_copy(tok.at[pl.ds(h * HALF, HALF), :], tslot(z, h), trecv.at[0, h]).wait()

        @pl.when(away)
        def _():
            wait_t(0, h)

    def start_both(pair_):
        pair_[0].start()
        pair_[1].start()

    def x_start(k):
        if k == 0:
            wait_w_local()
        else:
            wait_w(0, k, own[k])
        start_both(x_first(k))

    def x_forward(k):
        if k % 2 == 0:
            wait_w(1, k, shift(own[k], 3))
        else:
            wait_w(2, k, shift(own[k], 1))
        x_second(k).start()

    def duty(role, g, h):
        @pl.when(role)
        def _():
            if g == 0:
                wait_own_t(h)
                start_both(z_first(h))
            else:
                wait_t(g, h)
                if (g, h) in ((1, 0), (2, 1)):
                    z_second(h).start()
            to_partner(g, h).start()

    def ready(role, g):
        @pl.when(role)
        def _():
            for h in range(2):
                there = tbuf.at[(1 - c) * 4 + zs[g], pl.ds(h * HALF, HALF), :]
                send(there, there, psend.at[g, h], precv.at[g, h], partner).wait_recv()

    gain_row = gain[...].astype(jnp.float32).reshape(1, D)

    def norm(plane, g):
        block = plane * 4 + zs[g]

        def norm_rows(i, carry):
            rows = tbuf[block, pl.ds(pl.multiple_of(i * NCHUNK, NCHUNK), NCHUNK), :].astype(jnp.float32)
            scale = lax.rsqrt(jnp.mean(rows * rows, axis=1, keepdims=True) + 1e-05)
            to = pl.ds(pl.multiple_of(block * ROWS + i * NCHUNK, NCHUNK), NCHUNK)
            nbuf[to, :] = (rows * scale * gain_row).astype(jnp.bfloat16)
            return carry

        lax.fori_loop(0, ROWS // NCHUNK, norm_rows, 0)

    def turned(lin, rows):
        cosine, sine = cosb[rows, :], sinb[rows, :]
        parts = []
        for h in range(2):
            v = lin[:, h * HD : (h + 1) * HD]
            parts.append((v * cosine + pltpu.roll(v, HD // 2, 1) * sine).astype(jnp.bfloat16))
        return parts

    def project(first):
        rows = pl.ds(pl.multiple_of(first * ROWS, ROWS), ROWS)
        block = nbuf[rows, :]
        q = jnp.dot(block, wbuf[0], preferred_element_type=jnp.float32)
        for h, part in enumerate(turned(q, rows)):
            qbuf[h, rows, :] = part
        k = jnp.dot(block, wbuf[1], preferred_element_type=jnp.float32)
        for h, part in enumerate(turned(k, rows)):
            kbuf[h, rows, :] = part
        v = jnp.dot(block, wbuf[2], preferred_element_type=jnp.float32).astype(jnp.bfloat16)
        for h in range(2):
            vbuf[h, rows, :] = v[:, h * HD : (h + 1) * HD]

    def project_some(plane, groups):
        lo, hi = groups

        def one(g, carry):
            z_ = lax.rem(z + jnp.where(g == 0, 0, jnp.where(g == 1, 3, jnp.where(g == 2, 1, 2))), 4)
            project(plane * 4 + z_)
            return carry

        lax.fori_loop(lo, hi, one, 0)

    x_start(0)
    duty(home, 0, 0)
    duty(home, 0, 1)
    x_start(1)
    ready(away, 0)
    norm(yh, 0)
    x_start(2)
    x_start(3)
    duty(away, 0, 0)
    x_forward(0)
    duty(home, 1, 0)
    x_forward(1)
    duty(home, 2, 1)
    duty(home, 1, 1)
    duty(home, 2, 0)
    duty(away, 0, 1)
    ready(away, 1)
    norm(yh, 1)
    x_forward(2)
    ready(away, 2)
    norm(yh, 2)
    x_forward(3)
    duty(home, 3, 0)
    duty(home, 3, 1)
    ready(home, 0)
    norm(1 - yh, 0)
    ready(away, 3)
    norm(yh, 3)
    duty(away, 1, 0)
    duty(away, 2, 1)
    duty(away, 1, 1)
    duty(away, 2, 0)
    ready(home, 1)
    norm(1 - yh, 1)
    ready(home, 2)
    norm(1 - yh, 2)
    for k in (1, 3):
        wait_w(1, k, shift(own[k], 3))
    for k in (0, 2):
        wait_w(2, k, shift(own[k], 1))
    for k in range(4):
        wait_w(3, k, shift(own[k], 2))
    pltpu.make_async_copy(cos_hbm, cosb, lsem.at[0]).wait()
    pltpu.make_async_copy(sin_hbm, sinb, lsem.at[1]).wait()
    project_some(yh, (0, 4))
    duty(away, 3, 0)
    duty(away, 3, 1)
    project_some(1 - yh, (0, 3))
    ready(home, 3)
    norm(1 - yh, 3)
    project_some(1 - yh, (3, 4))

    factor = HD ** (-0.5) * math.log2(math.e)
    nt = (((1,), (1,)), ((), ()))
    rows_i = lax.broadcasted_iota(jnp.int32, (QB, QB), 0)
    cols_i = lax.broadcasted_iota(jnp.int32, (QB, QB), 1)
    allowed = cols_i <= rows_i
    mycols = pl.ds(pl.multiple_of(z * 512 + c * WC, WC), WC)

    def to_owner(b):
        return send(
            obuf.at[pl.ds(b * ROWS, ROWS), :], out.at[:, mycols], osend.at[b], orecv.at[z * 2 + c],
            dev(x, yl, yh, b // 4, b % 4),
        )

    def to_self(b):
        return pltpu.make_async_copy(obuf.at[pl.ds(b * ROWS, ROWS), :], out.at[:, mycols], osend.at[b])

    def own_block(b):
        return jnp.logical_and(home, t == b)

    sent = 0
    for j in range(NQ):

        def one_head(h, carry, j=j):
            q = qbuf[h, pl.ds(j * QB, QB), :]
            s_d = lax.dot_general(q, kbuf[h, pl.ds(j * QB, QB), :], nt, preferred_element_type=jnp.float32)
            s_d = jnp.where(allowed, s_d, -1e30)
            top = jnp.max(s_d, axis=1, keepdims=True)
            if j:
                s_p = lax.dot_general(q, kbuf[h, pl.ds(0, j * QB), :], nt, preferred_element_type=jnp.float32)
                top = jnp.maximum(top, jnp.max(s_p, axis=1, keepdims=True))
            e_d = jnp.exp2((s_d - top) * factor)
            total = jnp.sum(e_d, axis=1, keepdims=True)
            acc = jnp.dot(e_d.astype(jnp.bfloat16), vbuf[h, pl.ds(j * QB, QB), :], preferred_element_type=jnp.float32)
            if j:
                e_p = jnp.exp2((s_p - top) * factor)
                total = total + jnp.sum(e_p, axis=1, keepdims=True)
                acc = acc + jnp.dot(
                    e_p.astype(jnp.bfloat16), vbuf[h, pl.ds(0, j * QB), :], preferred_element_type=jnp.float32
                )
            obuf[pl.ds(j * QB, QB), pl.ds(pl.multiple_of(h * HD, HD), HD)] = (acc / total).astype(jnp.bfloat16)
            return carry

        lax.fori_loop(0, 2, one_head, 0)
        while sent < 8 and (sent + 1) * ROWS <= (j + 1) * QB:

            @pl.when(own_block(sent))
            def _(b=sent):
                to_self(b).start()

            @pl.when(jnp.logical_not(own_block(sent)))
            def _(b=sent):
                to_owner(b).start()

            sent += 1

    for z_ in range(4):
        for c_ in range(2):
            cols = pl.ds((z_ * 2 + c_) * WC, WC)
            mine = jnp.logical_and(home, jnp.logical_and(z == z_, c == c_))

            @pl.when(jnp.logical_not(mine))
            def _(i=z_ * 2 + c_, cols=cols):
                send(obuf.at[pl.ds(0, ROWS), :], out.at[:, cols], osend.at[0], orecv.at[i], partner).wait_recv()

    for b in range(8):

        @pl.when(own_block(b))
        def _(b=b):
            to_self(b).wait()

        @pl.when(jnp.logical_not(own_block(b)))
        def _(b=b):
            to_owner(b).wait_send()

    for i in range(3):
        send(wslot(d), wslot(d), wsend.at[0, i], wrecv.at[0, 0], partner).wait_send()
    for k in range(4):
        for copy in x_first(k):
            copy.wait_send()
        x_second(k).wait_send()
    for h in range(2):

        @pl.when(away)
        def _(h=h):
            exchange(h).wait_send()

        for copy in z_first(h):
            copy.wait_send()
        z_second(h).wait_send()
        for g in range(4):
            to_partner(g, h).wait_send()


def shards(tokens, norm_gain, q_weight, k_weight, v_weight):
    cosine, sine = tables()
    anywhere = pl.BlockSpec(memory_space=pl.ANY)
    bf, dma = jnp.bfloat16, pltpu.SemaphoreType.DMA
    attended = pl.pallas_call(
        kernel,
        out_shape=jax.ShapeDtypeStruct((ROWS, D), bf),
        in_specs=[anywhere, pl.BlockSpec(memory_space=pltpu.VMEM)] + [anywhere] * 5,
        out_specs=anywhere,
        scratch_shapes=[
            pltpu.VMEM((8, ROWS, D), bf),
            pltpu.VMEM((LEN, D), bf),
            pltpu.VMEM((3, D, WC), bf),
            pltpu.VMEM((2, LEN, HD), bf),
            pltpu.VMEM((2, LEN, HD), bf),
            pltpu.VMEM((2, LEN, HD), bf),
            pltpu.VMEM((LEN, WC), bf),
            pltpu.VMEM((LEN, HD), jnp.float32),
            pltpu.VMEM((LEN, HD), jnp.float32),
            dma((4, 4)),
            dma((4, 4)),
            dma((4, 2)),
            dma((4, 2)),
            dma((4, 2)),
            dma((4, 2)),
            dma((8,)),
            dma((8,)),
            dma((2,)),
        ],
        compiler_params=pltpu.CompilerParams(
            collective_id=0, has_side_effects=True, vmem_limit_bytes=60 * 2**20
        ),
        name="attention_block",
    )(tokens[0], norm_gain, q_weight, k_weight, v_weight, jnp.asarray(cosine), jnp.asarray(sine))
    return attended[None]


def solution(mesh):
    placed = (P("dp", "ctx", None), P(), P("dp", None), P("dp", None), P("dp", None))
    return jax.shard_map(
        shards, mesh=mesh, in_specs=placed, out_specs=P("dp", "ctx", None), check_vma=False
    )
```

```python
import functools
import math

import jax
import jax.numpy as jnp
import numpy as np
from jax import lax
from jax.experimental import pallas as pl
from jax.experimental.pallas import tpu as pltpu
from jax.sharding import PartitionSpec as P

MESH = pl.DeviceIdType.MESH
HEADS = 16
HD = 128
D = 2048
ROWS = 224
LEN = 1792
WR = 128
WC = 256
HALF = ROWS // 2
QB = 256
NQ = LEN // QB
NCHUNK = 16


def tables():
    freqs = 10000.0 ** (-2.0 * np.arange(HD // 2) / HD)
    angles = np.arange(LEN)[:, None] * freqs[None, :]
    cosine, sine = np.cos(angles), np.sin(angles)
    return (
        np.concatenate([cosine, cosine], axis=1).astype(np.float32),
        np.concatenate([-sine, sine], axis=1).astype(np.float32),
    )


def kernel(
    tok, gain, qw, kw, vw, cos_hbm, sin_hbm, out,
    tbuf, nbuf, wbuf, qbuf, kbuf, vbuf, obuf, cosb, sinb,
    yrecv, ysend, wrecv, wsend, trecv, tsend, precv, psend, osend, orecv, lsem,
):
    d, t = lax.axis_index("dp"), lax.axis_index("ctx")
    x, yl, c = d // 4, (d // 2) % 2, d % 2
    yh, z = t // 4, t % 4
    y = yh * 2 + yl
    home = c == yh
    away = c != yh

    def dev(x_, yl_, c_, yh_, z_):
        return (x_ * 4 + yl_ * 2 + c_, yh_ * 4 + z_)

    def chip_y(step, c_):
        y_ = (y + step) % 4
        return dev(x, y_ % 2, c_, y_ // 2, z)

    partner = dev(x, yl, 1 - c, yh, z)
    pair = dev(x, yl, 1 - c, 1 - yh, z)
    xp, xm = dev((x + 1) % 4, yl, c, yh, z), dev((x + 3) % 4, yl, c, yh, z)
    zp, zm = dev(x, yl, c, yh, (z + 1) % 4), dev(x, yl, c, yh, (z + 3) % 4)

    def send(src, dst, ss, rs, to):
        return pltpu.make_async_remote_copy(
            src_ref=src, dst_ref=dst, send_sem=ss, recv_sem=rs, device_id=to, device_id_type=MESH
        )

    def wslot(e):
        return wbuf.at[:, pl.ds(pl.multiple_of(e * WR, WR), WR), :]

    def wslot_one(i, e):
        return wbuf.at[i, pl.ds(pl.multiple_of(e * WR, WR), WR), :]

    def wcols(ref, c_):
        return ref.at[:, pl.ds(pl.multiple_of(z * 512 + c_ * WC, WC), WC)]

    def tslot(z_, h):
        return tbuf.at[c * 4 + z_, pl.ds(h * HALF, HALF), :]

    weights = (qw, kw, vw)
    for i, w in enumerate(weights):
        pltpu.make_async_copy(wcols(w, c), wslot_one(i, d), wrecv.at[0, 0]).start()

    @pl.when(home)
    def _():
        for h in range(2):
            pltpu.make_async_copy(tok.at[pl.ds(h * HALF, HALF), :], tslot(z, h), trecv.at[0, h]).start()

    pltpu.make_async_copy(cos_hbm, cosb, lsem.at[0]).start()
    pltpu.make_async_copy(sin_hbm, sinb, lsem.at[1]).start()

    barrier = pltpu.get_barrier_semaphore()

    def greet(to):
        pl.semaphore_signal(barrier, inc=1, device_id=to, device_id_type=MESH)

    for to in (partner, pair, xp, xm, zp, zm):
        greet(to)
    for step in (1, 3):
        for c_ in range(2):
            greet(chip_y(step, c_))
    pl.semaphore_wait(barrier, 10)

    for i, w in enumerate(weights):
        send(wcols(w, c), wslot_one(i, d), wsend.at[0, 0], wrecv.at[0, 2], chip_y(1, c)).start()
        send(wcols(w, 1 - c), wslot_one(i, d), wsend.at[0, 2], wrecv.at[0, 1], partner).start()

    def exchange(h):
        there = tbuf.at[(1 - c) * 4 + z, pl.ds(h * HALF, HALF), :]
        return send(tok.at[pl.ds(h * HALF, HALF), :], there, tsend.at[0, h], trecv.at[0, h], pair)

    @pl.when(away)
    def _():
        exchange(0).start()
        exchange(1).start()

    for i, w in enumerate(weights):
        send(wcols(w, 1 - c), wslot_one(i, d), wsend.at[0, 1], wrecv.at[0, 3], chip_y(3, 1 - c)).start()

    own = [d, x * 4 + yl * 2 + (1 - c), x * 4 + (1 - yl) * 2 + c, x * 4 + (1 - yl) * 2 + (1 - c)]

    def shift(e, s):
        return (e + 4 * s) % 16

    def wait_w(g, k, e):
        send(wslot(e), wslot(e), wsend.at[0, 0], wrecv.at[g, k], partner).wait_recv()

    def wait_w_local():
        for i, w in enumerate(weights):
            pltpu.make_async_copy(wcols(w, c), wslot_one(i, d), wrecv.at[0, 0]).wait()

    def x_first(k):
        e = own[k]
        return (
            send(wslot(e), wslot(e), wsend.at[1, k], wrecv.at[1, k], xp),
            send(wslot(e), wslot(e), wsend.at[2, k], wrecv.at[2, k], xm),
        )

    def wpart(e, h):
        return wbuf.at[:, pl.ds(pl.multiple_of(e * WR + h * (WR // 2), WR // 2), WR // 2), :]

    def x_second(k):
        if k == 0:
            e = shift(own[0], 3)
            return send(wslot(e), wslot(e), wsend.at[3, k], wrecv.at[3, k], xp)
        if k == 1:
            e = shift(own[1], 1)
            return send(wslot(e), wslot(e), wsend.at[3, k], wrecv.at[3, k], xm)
        e = shift(own[2], 3 if k == 2 else 1)
        return send(wpart(e, k - 2), wpart(e, k - 2), wsend.at[3, k], wrecv.at[3, k], xp if k == 2 else xm)

    def y_second(k):
        to = chip_y((1, 3)[k % 2], c)
        if k < 2:
            e = shift(own[1], (3, 1)[k])
            return send(wslot(e), wslot(e), ysend.at[k], yrecv.at[k], to)
        e = shift(own[1], 2)
        return send(wpart(e, k - 2), wpart(e, k - 2), ysend.at[k], yrecv.at[k], to)

    def z_first(h):
        return (
            send(tslot(z, h), tslot(z, h), tsend.at[1, h], trecv.at[1, h], zp),
            send(tslot(z, h), tslot(z, h), tsend.at[2, h], trecv.at[2, h], zm),
        )

    def z_second(h):
        z_ = (z + (3, 1)[h]) % 4
        return send(tslot(z_, h), tslot(z_, h), tsend.at[3, h], trecv.at[3, h], (zp, zm)[h])

    zs = [z, (z + 3) % 4, (z + 1) % 4, (z + 2) % 4]

    def to_partner(g, h):
        return send(tslot(zs[g], h), tslot(zs[g], h), psend.at[g, h], precv.at[g, h], partner)

    def wait_t(g, h):
        send(tslot(zs[g], h), tslot(zs[g], h), tsend.at[1, h], trecv.at[g, h], partner).wait_recv()

    def wait_own_t(h):
        @pl.when(home)
        def _():
            pltpu.make_async_copy(tok.at[pl.ds(h * HALF, HALF), :], tslot(z, h), trecv.at[0, h]).wait()

        @pl.when(away)
        def _():
            wait_t(0, h)

    def start_both(pair_):
        pair_[0].start()
        pair_[1].start()

    def x_start(k):
        if k == 0:
            wait_w_local()
        else:
            wait_w(0, k, own[k])
        start_both(x_first(k))

    def x_forward(k):
        wait_w(1 + k % 2, min(k, 2), shift(own[min(k, 2)], (3, 1)[k % 2]))
        x_second(k).start()

    def y_forward(k):
        if k == 0:
            wait_w(1, 1, shift(own[1], 3))
        if k == 2:
            wait_w(3, 1, shift(own[1], 2))
        y_second(k).start()

    def wait_rest_w():
        wait_w(2, 0, shift(own[0], 1))
        wait_w(3, 0, shift(own[0], 2))
        for h in range(2):
            there = wpart(shift(own[2], 2), h)
            send(there, there, wsend.at[0, 0], wrecv.at[3, 2 + h], partner).wait_recv()
        wait_w(0, 3, own[3])
        for k in range(4):
            there = wslot(shift(own[3], (3, 1)[k])) if k < 2 else wpart(shift(own[3], 2), k - 2)
            send(there, there, wsend.at[0, 0], yrecv.at[k], partner).wait_recv()

    def duty(role, g, h):
        @pl.when(role)
        def _():
            if g == 0:
                wait_own_t(h)
                start_both(z_first(h))
            else:
                wait_t(g, h)
                if (g, h) in ((1, 0), (2, 1)):
                    z_second(h).start()
            to_partner(g, h).start()

    def ready(role, g, halves=(0, 1)):
        @pl.when(role)
        def _():
            for h in halves:
                there = tbuf.at[(1 - c) * 4 + zs[g], pl.ds(h * HALF, HALF), :]
                send(there, there, psend.at[g, h], precv.at[g, h], partner).wait_recv()

    gain_row = gain[...].astype(jnp.float32).reshape(1, D)

    def norm(plane, g, halves=(0, 1)):
        block = plane * 4 + zs[g]

        def norm_rows(i, carry):
            rows = tbuf[block, pl.ds(pl.multiple_of(i * NCHUNK, NCHUNK), NCHUNK), :].astype(jnp.float32)
            scale = lax.rsqrt(jnp.mean(rows * rows, axis=1, keepdims=True) + 1e-05)
            to = pl.ds(pl.multiple_of(block * ROWS + i * NCHUNK, NCHUNK), NCHUNK)
            nbuf[to, :] = (rows * scale * gain_row).astype(jnp.bfloat16)
            return carry

        per = HALF // NCHUNK
        lax.fori_loop(halves[0] * per, (halves[-1] + 1) * per, norm_rows, 0, unroll=per)

    def turned(lin, rows):
        cosine, sine = cosb[rows, :], sinb[rows, :]
        parts = []
        for h in range(2):
            v = lin[:, h * HD : (h + 1) * HD]
            parts.append((v * cosine + pltpu.roll(v, HD // 2, 1) * sine).astype(jnp.bfloat16))
        return parts

    def project(first, blocks):
        rows = pl.ds(pl.multiple_of(first * ROWS, ROWS), blocks * ROWS)
        block = nbuf[rows, :]
        q = jnp.dot(block, wbuf[0], preferred_element_type=jnp.float32)
        for h, part in enumerate(turned(q, rows)):
            qbuf[h, rows, :] = part
        k = jnp.dot(block, wbuf[1], preferred_element_type=jnp.float32)
        for h, part in enumerate(turned(k, rows)):
            kbuf[h, rows, :] = part
        v = jnp.dot(block, wbuf[2], preferred_element_type=jnp.float32).astype(jnp.bfloat16)
        for h in range(2):
            vbuf[h, rows, :] = v[:, h * HD : (h + 1) * HD]

    x_start(0)
    duty(home, 0, 0)
    duty(home, 0, 1)
    x_start(1)
    ready(away, 0)
    norm(yh, 0)
    x_start(2)
    x_forward(0)
    duty(home, 1, 0)
    duty(home, 2, 0)
    duty(away, 0, 0)
    x_forward(1)
    y_forward(0)
    y_forward(1)
    duty(home, 2, 1)
    duty(home, 1, 1)
    duty(away, 0, 1)
    ready(away, 1)
    norm(yh, 1)
    x_forward(2)
    x_forward(3)
    ready(away, 2)
    norm(yh, 2)
    ready(home, 0)
    norm(1 - yh, 0)
    y_forward(2)
    y_forward(3)
    duty(away, 1, 0)
    duty(away, 2, 0)
    duty(home, 3, 0)
    duty(home, 3, 1)
    ready(away, 3)
    norm(yh, 3)
    wait_rest_w()
    pltpu.make_async_copy(cos_hbm, cosb, lsem.at[0]).wait()
    pltpu.make_async_copy(sin_hbm, sinb, lsem.at[1]).wait()
    project(yh * 4, 2)
    duty(away, 2, 1)
    duty(away, 1, 1)
    project(yh * 4 + 2, 2)
    ready(home, 1)
    norm(1 - yh, 1)
    ready(home, 2)
    norm(1 - yh, 2)
    project((1 - yh) * 4 + z - z % 2, 2)
    duty(away, 3, 0)
    project((1 - yh) * 4 + (z + jnp.where(z % 2 == 0, 3, 1)) % 4, 1)
    ready(home, 3, (0,))
    norm(1 - yh, 3, (0,))
    duty(away, 3, 1)
    ready(home, 3, (1,))
    norm(1 - yh, 3, (1,))
    project((1 - yh) * 4 + zs[3], 1)

    factor = HD ** (-0.5) * math.log2(math.e)
    nt = (((1,), (1,)), ((), ()))
    rows_i = lax.broadcasted_iota(jnp.int32, (QB, QB), 0)
    cols_i = lax.broadcasted_iota(jnp.int32, (QB, QB), 1)
    allowed = cols_i <= rows_i
    mycols = pl.ds(pl.multiple_of(z * 512 + c * WC, WC), WC)

    def to_owner(b):
        return send(
            obuf.at[pl.ds(b * ROWS, ROWS), :], out.at[:, mycols], osend.at[b], orecv.at[z * 2 + c],
            dev(x, yl, yh, b // 4, b % 4),
        )

    def to_self(b):
        return pltpu.make_async_copy(obuf.at[pl.ds(b * ROWS, ROWS), :], out.at[:, mycols], osend.at[b])

    def own_block(b):
        return jnp.logical_and(home, t == b)

    sent = 0
    for j in range(NQ):

        def one_head(h, carry, j=j):
            q = qbuf[h, pl.ds(j * QB, QB), :]
            s_d = lax.dot_general(q, kbuf[h, pl.ds(j * QB, QB), :], nt, preferred_element_type=jnp.float32)
            s_d = jnp.where(allowed, s_d, -1e30)
            top = jnp.max(s_d, axis=1, keepdims=True)
            if j:
                s_p = lax.dot_general(q, kbuf[h, pl.ds(0, j * QB), :], nt, preferred_element_type=jnp.float32)
                top = jnp.maximum(top, jnp.max(s_p, axis=1, keepdims=True))
            e_d = jnp.exp2((s_d - top) * factor)
            total = jnp.sum(e_d, axis=1, keepdims=True)
            acc = jnp.dot(e_d.astype(jnp.bfloat16), vbuf[h, pl.ds(j * QB, QB), :], preferred_element_type=jnp.float32)
            if j:
                e_p = jnp.exp2((s_p - top) * factor)
                total = total + jnp.sum(e_p, axis=1, keepdims=True)
                acc = acc + jnp.dot(
                    e_p.astype(jnp.bfloat16), vbuf[h, pl.ds(0, j * QB), :], preferred_element_type=jnp.float32
                )
            obuf[pl.ds(j * QB, QB), pl.ds(pl.multiple_of(h * HD, HD), HD)] = (acc / total).astype(jnp.bfloat16)
            return carry

        lax.fori_loop(0, 2, one_head, 0, unroll=True)
        while sent < 8 and (sent + 1) * ROWS <= (j + 1) * QB:

            @pl.when(own_block(sent))
            def _(b=sent):
                to_self(b).start()

            @pl.when(jnp.logical_not(own_block(sent)))
            def _(b=sent):
                to_owner(b).start()

            sent += 1

    for z_ in range(4):
        for c_ in range(2):
            cols = pl.ds((z_ * 2 + c_) * WC, WC)
            mine = jnp.logical_and(home, jnp.logical_and(z == z_, c == c_))

            @pl.when(jnp.logical_not(mine))
            def _(i=z_ * 2 + c_, cols=cols):
                send(obuf.at[pl.ds(0, ROWS), :], out.at[:, cols], osend.at[0], orecv.at[i], partner).wait_recv()

    for b in range(8):

        @pl.when(own_block(b))
        def _(b=b):
            to_self(b).wait()

        @pl.when(jnp.logical_not(own_block(b)))
        def _(b=b):
            to_owner(b).wait_send()

    for i in range(3):
        send(wslot(d), wslot(d), wsend.at[0, i], wrecv.at[0, 0], partner).wait_send()
    for k in range(4):
        if k < 3:
            for copy in x_first(k):
                copy.wait_send()
        x_second(k).wait_send()
        y_second(k).wait_send()
    for h in range(2):

        @pl.when(away)
        def _(h=h):
            exchange(h).wait_send()

        for copy in z_first(h):
            copy.wait_send()
        z_second(h).wait_send()
        for g in range(4):
            to_partner(g, h).wait_send()


def shards(tokens, norm_gain, q_weight, k_weight, v_weight):
    cosine, sine = tables()
    anywhere = pl.BlockSpec(memory_space=pl.ANY)
    bf, dma = jnp.bfloat16, pltpu.SemaphoreType.DMA
    attended = pl.pallas_call(
        kernel,
        out_shape=jax.ShapeDtypeStruct((ROWS, D), bf),
        in_specs=[anywhere, pl.BlockSpec(memory_space=pltpu.VMEM)] + [anywhere] * 5,
        out_specs=anywhere,
        scratch_shapes=[
            pltpu.VMEM((8, ROWS, D), bf),
            pltpu.VMEM((LEN, D), bf),
            pltpu.VMEM((3, D, WC), bf),
            pltpu.VMEM((2, LEN, HD), bf),
            pltpu.VMEM((2, LEN, HD), bf),
            pltpu.VMEM((2, LEN, HD), bf),
            pltpu.VMEM((LEN, WC), bf),
            pltpu.VMEM((LEN, HD), jnp.float32),
            pltpu.VMEM((LEN, HD), jnp.float32),
            dma((4,)),
            dma((4,)),
            dma((4, 4)),
            dma((4, 4)),
            dma((4, 2)),
            dma((4, 2)),
            dma((4, 2)),
            dma((4, 2)),
            dma((8,)),
            dma((8,)),
            dma((2,)),
        ],
        compiler_params=pltpu.CompilerParams(
            collective_id=0, has_side_effects=True, vmem_limit_bytes=60 * 2**20
        ),
        name="attention_block",
    )(tokens[0], norm_gain, q_weight, k_weight, v_weight, jnp.asarray(cosine), jnp.asarray(sine))
    return attended[None]


def solution(mesh):
    placed = (P("dp", "ctx", None), P(), P("dp", None), P("dp", None), P("dp", None))
    return jax.shard_map(
        shards, mesh=mesh, in_specs=placed, out_specs=P("dp", "ctx", None), check_vma=False
    )
```

```python
import functools
import math

import jax
import jax.numpy as jnp
import numpy as np
from jax import lax
from jax.experimental import pallas as pl
from jax.experimental.pallas import tpu as pltpu
from jax.sharding import PartitionSpec as P

MESH = pl.DeviceIdType.MESH
HEADS = 16
HD = 128
D = 2048
ROWS = 224
LEN = 1792
WR = 128
WC = 256
QB = 256
NQ = LEN // QB
PIECES = ((0, 64), (64, 48), (112, 64), (176, 48))
NCHUNK = 16


def tables():
    freqs = 10000.0 ** (-2.0 * np.arange(HD // 2) / HD)
    angles = np.arange(LEN)[:, None] * freqs[None, :]
    cosine, sine = np.cos(angles), np.sin(angles)
    return (
        np.concatenate([cosine, cosine], axis=1).astype(np.float32),
        np.concatenate([-sine, sine], axis=1).astype(np.float32),
    )


def kernel(
    tok, gain, qw, kw, vw, cos_hbm, sin_hbm, out,
    tbuf, nbuf, wbuf, lin, qbuf, kbuf, vbuf, obuf, cosb, sinb,
    yrecv, ysend, wrecv, wsend, trecv, tsend, precv, psend, osend, orecv, lsem,
):
    d, t = lax.axis_index("dp"), lax.axis_index("ctx")
    x, yl, c = d // 4, (d // 2) % 2, d % 2
    yh, z = t // 4, t % 4
    y = yh * 2 + yl
    home = c == yh
    away = c != yh

    def dev(x_, yl_, c_, yh_, z_):
        return (x_ * 4 + yl_ * 2 + c_, yh_ * 4 + z_)

    def chip_y(step, c_):
        y_ = (y + step) % 4
        return dev(x, y_ % 2, c_, y_ // 2, z)

    partner = dev(x, yl, 1 - c, yh, z)
    pair = dev(x, yl, 1 - c, 1 - yh, z)
    xp, xm = dev((x + 1) % 4, yl, c, yh, z), dev((x + 3) % 4, yl, c, yh, z)
    zp, zm = dev(x, yl, c, yh, (z + 1) % 4), dev(x, yl, c, yh, (z + 3) % 4)

    def send(src, dst, ss, rs, to):
        return pltpu.make_async_remote_copy(
            src_ref=src, dst_ref=dst, send_sem=ss, recv_sem=rs, device_id=to, device_id_type=MESH
        )

    def wslot(e):
        return wbuf.at[:, pl.ds(pl.multiple_of(e * WR, WR), WR), :]

    def wslot_one(i, e):
        return wbuf.at[i, pl.ds(pl.multiple_of(e * WR, WR), WR), :]

    def wcols(ref, c_):
        return ref.at[:, pl.ds(pl.multiple_of(z * 512 + c_ * WC, WC), WC)]

    def rows_of(i):
        return pl.ds(*PIECES[i])

    def tslot(z_, h):
        return tbuf.at[c * 4 + z_, rows_of(h), :]

    weights = (qw, kw, vw)
    for i, w in enumerate(weights):
        pltpu.make_async_copy(wcols(w, c), wslot_one(i, d), wrecv.at[0, 0]).start()

    @pl.when(home)
    def _():
        for h in range(4):
            pltpu.make_async_copy(tok.at[rows_of(h), :], tslot(z, h), trecv.at[0, h]).start()

    pltpu.make_async_copy(cos_hbm, cosb, lsem.at[0]).start()
    pltpu.make_async_copy(sin_hbm, sinb, lsem.at[1]).start()

    barrier = pltpu.get_barrier_semaphore()

    def greet(to):
        pl.semaphore_signal(barrier, inc=1, device_id=to, device_id_type=MESH)

    for to in (partner, pair, xp, xm, zp, zm):
        greet(to)
    for step in (1, 3):
        for c_ in range(2):
            greet(chip_y(step, c_))
    pl.semaphore_wait(barrier, 10)

    for i, w in enumerate(weights):
        send(wcols(w, c), wslot_one(i, d), wsend.at[0, 0], wrecv.at[0, 2], chip_y(1, c)).start()
        send(wcols(w, 1 - c), wslot_one(i, d), wsend.at[0, 2], wrecv.at[0, 1], partner).start()

    def exchange(h):
        there = tbuf.at[(1 - c) * 4 + z, rows_of(h), :]
        return send(tok.at[rows_of(h), :], there, tsend.at[0, h], trecv.at[0, h], pair)

    @pl.when(away)
    def _():
        for h in (0, 2, 1, 3):
            exchange(h).start()

    for i, w in enumerate(weights):
        send(wcols(w, 1 - c), wslot_one(i, d), wsend.at[0, 1], wrecv.at[0, 3], chip_y(3, 1 - c)).start()

    own = [d, x * 4 + yl * 2 + (1 - c), x * 4 + (1 - yl) * 2 + c, x * 4 + (1 - yl) * 2 + (1 - c)]

    def shift(e, s):
        return (e + 4 * s) % 16

    def wait_w(g, k, e):
        send(wslot(e), wslot(e), wsend.at[0, 0], wrecv.at[g, k], partner).wait_recv()

    def wait_w_local():
        for i, w in enumerate(weights):
            pltpu.make_async_copy(wcols(w, c), wslot_one(i, d), wrecv.at[0, 0]).wait()

    def x_first(k):
        e = own[k]
        return (
            send(wslot(e), wslot(e), wsend.at[1, k], wrecv.at[1, k], xp),
            send(wslot(e), wslot(e), wsend.at[2, k], wrecv.at[2, k], xm),
        )

    def wpart(e, h):
        return wbuf.at[:, pl.ds(pl.multiple_of(e * WR + h * (WR // 2), WR // 2), WR // 2), :]

    def x_second(k):
        if k == 0:
            e = shift(own[0], 3)
            return send(wslot(e), wslot(e), wsend.at[3, k], wrecv.at[3, k], xp)
        if k == 1:
            e = shift(own[1], 1)
            return send(wslot(e), wslot(e), wsend.at[3, k], wrecv.at[3, k], xm)
        e = shift(own[2], 3 if k == 2 else 1)
        return send(wpart(e, k - 2), wpart(e, k - 2), wsend.at[3, k], wrecv.at[3, k], xp if k == 2 else xm)

    def y_second(k):
        to = chip_y((1, 3)[k % 2], c)
        if k < 2:
            e = shift(own[1], (3, 1)[k])
            return send(wslot(e), wslot(e), ysend.at[k], yrecv.at[k], to)
        e = shift(own[1], 2)
        return send(wpart(e, k - 2), wpart(e, k - 2), ysend.at[k], yrecv.at[k], to)

    def z_first(h):
        return (
            send(tslot(z, h), tslot(z, h), tsend.at[1, h], trecv.at[1, h], zp),
            send(tslot(z, h), tslot(z, h), tsend.at[2, h], trecv.at[2, h], zm),
        )

    def z_second(h):
        z_ = (z + (3, 1)[h // 2]) % 4
        return send(tslot(z_, h), tslot(z_, h), tsend.at[3, h], trecv.at[3, h], (zp, zm)[h // 2])

    zs = [z, (z + 3) % 4, (z + 1) % 4, (z + 2) % 4]

    def to_partner(g, h):
        return send(tslot(zs[g], h), tslot(zs[g], h), psend.at[g, h], precv.at[g, h], partner)

    def wait_t(g, h):
        send(tslot(zs[g], h), tslot(zs[g], h), tsend.at[1, h], trecv.at[g, h], partner).wait_recv()

    def wait_own_t(h):
        @pl.when(home)
        def _():
            pltpu.make_async_copy(tok.at[rows_of(h), :], tslot(z, h), trecv.at[0, h]).wait()

        @pl.when(away)
        def _():
            wait_t(0, h)

    def start_both(pair_):
        pair_[0].start()
        pair_[1].start()

    def x_start(k):
        if k == 0:
            wait_w_local()
        else:
            wait_w(0, k, own[k])
        start_both(x_first(k))

    def x_forward(k):
        wait_w(1 + k % 2, min(k, 2), shift(own[min(k, 2)], (3, 1)[k % 2]))
        x_second(k).start()

    def y_forward(k):
        if k == 0:
            wait_w(1, 1, shift(own[1], 3))
        if k == 2:
            wait_w(3, 1, shift(own[1], 2))
        y_second(k).start()

    def wait_y(k):
        there = wslot(shift(own[3], (3, 1)[k])) if k < 2 else wpart(shift(own[3], 2), k - 2)
        send(there, there, wsend.at[0, 0], yrecv.at[k], partner).wait_recv()

    def wait_nearby_w():
        wait_w(2, 0, shift(own[0], 1))
        wait_w(0, 3, own[3])
        wait_y(0)
        wait_y(1)

    def wait_across_w():
        wait_w(3, 0, shift(own[0], 2))
        for h in range(2):
            there = wpart(shift(own[2], 2), h)
            send(there, there, wsend.at[0, 0], wrecv.at[3, 2 + h], partner).wait_recv()
        wait_y(2)
        wait_y(3)

    def duty(role, g, h):
        @pl.when(role)
        def _():
            if g == 0:
                wait_own_t(h)
                z_first(h)[h // 2].start()
                if h == 3:
                    z_first(2)[0].start()
                    z_first(0)[1].start()
                    z_first(3)[0].start()
                    z_first(1)[1].start()
            else:
                wait_t(g, h)
                if (g, h // 2) in ((1, 0), (2, 1)):
                    z_second(h).start()
            to_partner(g, h).start()

    def ready(role, g, pieces=(0, 1, 2, 3)):
        @pl.when(role)
        def _():
            for h in pieces:
                there = tbuf.at[(1 - c) * 4 + zs[g], rows_of(h), :]
                send(there, there, psend.at[g, h], precv.at[g, h], partner).wait_recv()

    gain_row = gain[...].astype(jnp.float32).reshape(1, D)

    def norm(plane, g, pieces=(0, 3)):
        block = plane * 4 + zs[g]

        def norm_rows(i, carry):
            rows = tbuf[block, pl.ds(pl.multiple_of(i * NCHUNK, NCHUNK), NCHUNK), :].astype(jnp.float32)
            scale = lax.rsqrt(jnp.mean(rows * rows, axis=1, keepdims=True) + 1e-05)
            to = pl.ds(pl.multiple_of(block * ROWS + i * NCHUNK, NCHUNK), NCHUNK)
            nbuf[to, :] = (rows * scale * gain_row).astype(jnp.bfloat16)
            return carry

        lo, hi = PIECES[pieces[0]][0] // NCHUNK, sum(PIECES[pieces[1]]) // NCHUNK
        lax.fori_loop(lo, hi, norm_rows, 0, unroll=7)

    def turned(product, rows):
        cosine, sine = cosb[rows, :], sinb[rows, :]
        parts = []
        for h in range(2):
            v = product[:, h * HD : (h + 1) * HD]
            parts.append((v * cosine + pltpu.roll(v, HD // 2, 1) * sine).astype(jnp.bfloat16))
        return parts

    def dots(rows, i, chips):
        total = None
        for x_ in chips:
            depth = pl.ds(pl.multiple_of(x_ * 4 * WR, 4 * WR), 4 * WR)
            part = jnp.dot(nbuf[rows, depth], wbuf[i, depth, :], preferred_element_type=jnp.float32)
            total = part if total is None else total + part
        return total

    nearby, across = (x, (x + 3) % 4, (x + 1) % 4), (x + 2) % 4

    def project_nearby(first, local):
        rows = pl.ds(pl.multiple_of(first * ROWS, ROWS), 2 * ROWS)
        for i in range(3):
            lin[i, pl.ds(local * ROWS, 2 * ROWS), :] = dots(rows, i, nearby)

    def project(first, blocks, local=None):
        rows = pl.ds(pl.multiple_of(first * ROWS, ROWS), blocks * ROWS)

        def product(i):
            if local is None:
                return jnp.dot(nbuf[rows, :], wbuf[i], preferred_element_type=jnp.float32)
            return lin[i, pl.ds(local * ROWS, blocks * ROWS), :] + dots(rows, i, (across,))

        for buf, i in ((qbuf, 0), (kbuf, 1)):
            for h, part in enumerate(turned(product(i), rows)):
                buf[h, rows, :] = part
        v = product(2).astype(jnp.bfloat16)
        for h in range(2):
            vbuf[h, rows, :] = v[:, h * HD : (h + 1) * HD]

    def duties(role, g, pieces):
        for h in pieces:
            duty(role, g, h)

    x_start(0)
    duties(home, 0, (0, 2, 1, 3))
    x_start(1)
    ready(away, 0)
    norm(yh, 0)
    duty(home, 1, 0)
    duty(home, 2, 2)
    x_start(2)
    x_forward(0)
    duty(home, 1, 1)
    duty(home, 2, 3)
    x_forward(1)
    y_forward(0)
    y_forward(1)
    duty(away, 0, 0)
    duty(away, 0, 2)
    duties(home, 2, (0, 1))
    duties(home, 1, (2, 3))
    x_forward(2)
    x_forward(3)
    duties(away, 0, (1, 3))
    ready(away, 1)
    norm(yh, 1)
    ready(away, 2)
    norm(yh, 2)
    duty(away, 1, 0)
    duty(away, 2, 2)
    y_forward(2)
    y_forward(3)
    duties(home, 3, (0, 2, 1, 3))
    ready(home, 0)
    norm(1 - yh, 0)
    ready(away, 3)
    norm(yh, 3)
    duty(away, 1, 1)
    duty(away, 2, 3)
    wait_nearby_w()
    pltpu.make_async_copy(cos_hbm, cosb, lsem.at[0]).wait()
    pltpu.make_async_copy(sin_hbm, sinb, lsem.at[1]).wait()
    project_nearby(yh * 4, 0)
    project_nearby(yh * 4 + 2, 2)
    wait_across_w()
    project(yh * 4, 2, 0)
    duties(away, 1, (2, 3))
    duties(away, 2, (0, 1))
    project(yh * 4 + 2, 2, 2)
    ready(home, 1)
    norm(1 - yh, 1)
    ready(home, 2)
    norm(1 - yh, 2)
    project((1 - yh) * 4 + z - z % 2, 2)
    duty(away, 3, 0)
    duty(away, 3, 2)
    project((1 - yh) * 4 + (z + jnp.where(z % 2 == 0, 3, 1)) % 4, 1)
    duty(away, 3, 1)
    ready(home, 3, (0, 1))
    norm(1 - yh, 3, (0, 1))
    duty(away, 3, 3)
    ready(home, 3, (2, 3))
    norm(1 - yh, 3, (2, 3))
    project((1 - yh) * 4 + zs[3], 1)

    factor = HD ** (-0.5) * math.log2(math.e)
    nt = (((1,), (1,)), ((), ()))
    rows_i = lax.broadcasted_iota(jnp.int32, (QB, QB), 0)
    cols_i = lax.broadcasted_iota(jnp.int32, (QB, QB), 1)
    allowed = cols_i <= rows_i
    mycols = pl.ds(pl.multiple_of(z * 512 + c * WC, WC), WC)

    def parts(j):
        found = []
        for b in range(8):
            lo, hi = max(b * ROWS, j * QB), min((b + 1) * ROWS, (j + 1) * QB)
            if lo < hi:
                found.append((b, lo - b * ROWS, lo, hi - lo))
        return found

    def to_owner(b, first, row, n):
        return send(
            obuf.at[pl.ds(row, n), :], out.at[pl.ds(first, n), mycols], osend.at[b], orecv.at[z * 2 + c],
            dev(x, yl, yh, b // 4, b % 4),
        )

    def to_self(b, first, row, n):
        return pltpu.make_async_copy(obuf.at[pl.ds(row, n), :], out.at[pl.ds(first, n), mycols], osend.at[b])

    def own_block(b):
        return jnp.logical_and(home, t == b)

    def attend(b, h):
        rows, past = pl.ds(b * QB, QB), pl.ds(0, b * QB)
        q = qbuf[h, rows, :]
        s_d = lax.dot_general(q, kbuf[h, rows, :], nt, preferred_element_type=jnp.float32)
        s_d = jnp.where(allowed, s_d, -1e30)
        top = jnp.max(s_d, axis=1, keepdims=True)
        if b:
            s_p = lax.dot_general(q, kbuf[h, past, :], nt, preferred_element_type=jnp.float32)
            top = jnp.maximum(top, jnp.max(s_p, axis=1, keepdims=True))
        e_d = jnp.exp2((s_d - top) * factor)
        total = jnp.sum(e_d, axis=1, keepdims=True)
        acc = jnp.dot(e_d.astype(jnp.bfloat16), vbuf[h, rows, :], preferred_element_type=jnp.float32)
        if b:
            e_p = jnp.exp2((s_p - top) * factor)
            total = total + jnp.sum(e_p, axis=1, keepdims=True)
            acc = acc + jnp.dot(e_p.astype(jnp.bfloat16), vbuf[h, past, :], preferred_element_type=jnp.float32)
        obuf[rows, h * HD : (h + 1) * HD] = (acc / total).astype(jnp.bfloat16)

    def one_block(i, carry):
        far = (z + 2) % 4
        near = far - jnp.where(far > 1, 1, 0)
        j_ = jnp.where(i < 4, (1 - yh) * 3 + (far + i) % 4, yh * 4 + (near + i - 4) % 3)
        for j in range(NQ):

            @pl.when(j_ == j)
            def _(j=j):
                for h in range(2):
                    attend(j, h)
                for part in parts(j):

                    @pl.when(own_block(part[0]))
                    def _(part=part):
                        to_self(*part).start()

                    @pl.when(jnp.logical_not(own_block(part[0])))
                    def _(part=part):
                        to_owner(*part).start()

        return carry

    lax.fori_loop(0, NQ, one_block, 0)

    for z_ in range(4):
        for c_ in range(2):
            cols = pl.ds((z_ * 2 + c_) * WC, WC)
            mine = jnp.logical_and(home, jnp.logical_and(z == z_, c == c_))

            @pl.when(jnp.logical_not(mine))
            def _(i=z_ * 2 + c_, cols=cols):
                send(obuf.at[pl.ds(0, ROWS), :], out.at[:, cols], osend.at[0], orecv.at[i], partner).wait_recv()

    for b in range(8):

        @pl.when(own_block(b))
        def _(b=b):
            to_self(b, 0, b * ROWS, ROWS).wait()

        @pl.when(jnp.logical_not(own_block(b)))
        def _(b=b):
            to_owner(b, 0, b * ROWS, ROWS).wait_send()

    for i in range(3):
        send(wslot(d), wslot(d), wsend.at[0, i], wrecv.at[0, 0], partner).wait_send()
    for k in range(4):
        if k < 3:
            for copy in x_first(k):
                copy.wait_send()
        x_second(k).wait_send()
        y_second(k).wait_send()
    for h in range(4):

        @pl.when(away)
        def _(h=h):
            exchange(h).wait_send()

        for copy in z_first(h):
            copy.wait_send()
        z_second(h).wait_send()
        for g in range(4):
            to_partner(g, h).wait_send()


def shards(tokens, norm_gain, q_weight, k_weight, v_weight):
    cosine, sine = tables()
    anywhere = pl.BlockSpec(memory_space=pl.ANY)
    bf, dma = jnp.bfloat16, pltpu.SemaphoreType.DMA
    attended = pl.pallas_call(
        kernel,
        out_shape=jax.ShapeDtypeStruct((ROWS, D), bf),
        in_specs=[anywhere, pl.BlockSpec(memory_space=pltpu.VMEM)] + [anywhere] * 5,
        out_specs=anywhere,
        scratch_shapes=[
            pltpu.VMEM((8, ROWS, D), bf),
            pltpu.VMEM((LEN, D), bf),
            pltpu.VMEM((3, D, WC), bf),
            pltpu.VMEM((3, 4 * ROWS, WC), jnp.float32),
            pltpu.VMEM((2, LEN, HD), bf),
            pltpu.VMEM((2, LEN, HD), bf),
            pltpu.VMEM((2, LEN, HD), bf),
            pltpu.VMEM((LEN, WC), bf),
            pltpu.VMEM((LEN, HD), jnp.float32),
            pltpu.VMEM((LEN, HD), jnp.float32),
            dma((4,)),
            dma((4,)),
            dma((4, 4)),
            dma((4, 4)),
            dma((4, 4)),
            dma((4, 4)),
            dma((4, 4)),
            dma((4, 4)),
            dma((8,)),
            dma((8,)),
            dma((2,)),
        ],
        compiler_params=pltpu.CompilerParams(
            collective_id=0, has_side_effects=True, vmem_limit_bytes=60 * 2**20
        ),
        name="attention_block",
    )(tokens[0], norm_gain, q_weight, k_weight, v_weight, jnp.asarray(cosine), jnp.asarray(sine))
    return attended[None]


def solution(mesh):
    placed = (P("dp", "ctx", None), P(), P("dp", None), P("dp", None), P("dp", None))
    return jax.shard_map(
        shards, mesh=mesh, in_specs=placed, out_specs=P("dp", "ctx", None), check_vma=False
    )
```

```python
import functools
import math

import jax
import jax.numpy as jnp
import numpy as np
from jax import lax
from jax.experimental import pallas as pl
from jax.experimental.pallas import tpu as pltpu
from jax.sharding import PartitionSpec as P

MESH = pl.DeviceIdType.MESH
HEADS = 16
HD = 128
D = 2048
ROWS = 224
LEN = 1792
WR = 128
WC = 256
QB = 256
NQ = LEN // QB
PIECES = ((0, 64), (64, 48), (112, 64), (176, 48))
NCHUNK = 16


def tables():
    freqs = 10000.0 ** (-2.0 * np.arange(HD // 2) / HD)
    angles = np.arange(LEN)[:, None] * freqs[None, :]
    cosine, sine = np.cos(angles), np.sin(angles)
    return (
        np.concatenate([cosine, cosine], axis=1).astype(np.float32),
        np.concatenate([-sine, sine], axis=1).astype(np.float32),
    )


def kernel(
    tok, gain, qw, kw, vw, cos_hbm, sin_hbm, out,
    tbuf, nbuf, wbuf, lin, qbuf, kbuf, vbuf, obuf, cosb, sinb,
    yrecv, ysend, wrecv, wsend, trecv, tsend, precv, psend, osend, orecv, lsem,
):
    d, t = lax.axis_index("dp"), lax.axis_index("ctx")
    x, yl, c = d // 4, (d // 2) % 2, d % 2
    yh, z = t // 4, t % 4
    y = yh * 2 + yl
    home = c == yh
    away = c != yh

    def dev(x_, yl_, c_, yh_, z_):
        return (x_ * 4 + yl_ * 2 + c_, yh_ * 4 + z_)

    def chip_y(step, c_):
        y_ = (y + step) % 4
        return dev(x, y_ % 2, c_, y_ // 2, z)

    partner = dev(x, yl, 1 - c, yh, z)
    pair = dev(x, yl, 1 - c, 1 - yh, z)
    xp, xm = dev((x + 1) % 4, yl, c, yh, z), dev((x + 3) % 4, yl, c, yh, z)
    zp, zm = dev(x, yl, c, yh, (z + 1) % 4), dev(x, yl, c, yh, (z + 3) % 4)

    def send(src, dst, ss, rs, to):
        return pltpu.make_async_remote_copy(
            src_ref=src, dst_ref=dst, send_sem=ss, recv_sem=rs, device_id=to, device_id_type=MESH
        )

    def wslot(e):
        return wbuf.at[:, pl.ds(pl.multiple_of(e * WR, WR), WR), :]

    def wslot_one(i, e):
        return wbuf.at[i, pl.ds(pl.multiple_of(e * WR, WR), WR), :]

    def wcols(ref, c_):
        return ref.at[:, pl.ds(pl.multiple_of(z * 512 + c_ * WC, WC), WC)]

    def rows_of(i):
        return pl.ds(*PIECES[i])

    def tslot(z_, h):
        return tbuf.at[c * 4 + z_, rows_of(h), :]

    weights = (qw, kw, vw)
    for i, w in enumerate(weights):
        pltpu.make_async_copy(wcols(w, c), wslot_one(i, d), wrecv.at[0, 0]).start()

    @pl.when(home)
    def _():
        for h in range(4):
            pltpu.make_async_copy(tok.at[rows_of(h), :], tslot(z, h), trecv.at[0, h]).start()

    pltpu.make_async_copy(cos_hbm, cosb, lsem.at[0]).start()
    pltpu.make_async_copy(sin_hbm, sinb, lsem.at[1]).start()

    barrier = pltpu.get_barrier_semaphore()

    def greet(to):
        pl.semaphore_signal(barrier, inc=1, device_id=to, device_id_type=MESH)

    for to in (partner, pair, xp, xm, zp, zm):
        greet(to)
    for step in (1, 3):
        for c_ in range(2):
            greet(chip_y(step, c_))
    pl.semaphore_wait(barrier, 10)

    for i, w in enumerate(weights):
        send(wcols(w, c), wslot_one(i, d), wsend.at[0, 0], wrecv.at[0, 2], chip_y(1, c)).start()
        send(wcols(w, 1 - c), wslot_one(i, d), wsend.at[0, 2], wrecv.at[0, 1], partner).start()

    def exchange(h):
        there = tbuf.at[(1 - c) * 4 + z, rows_of(h), :]
        return send(tok.at[rows_of(h), :], there, tsend.at[0, h], trecv.at[0, h], pair)

    @pl.when(away)
    def _():
        for h in (0, 2, 1, 3):
            exchange(h).start()

    for i, w in enumerate(weights):
        send(wcols(w, 1 - c), wslot_one(i, d), wsend.at[0, 1], wrecv.at[0, 3], chip_y(3, 1 - c)).start()

    own = [d, x * 4 + yl * 2 + (1 - c), x * 4 + (1 - yl) * 2 + c, x * 4 + (1 - yl) * 2 + (1 - c)]

    def shift(e, s):
        return (e + 4 * s) % 16

    def wait_w(g, k, e):
        send(wslot(e), wslot(e), wsend.at[0, 0], wrecv.at[g, k], partner).wait_recv()

    def wait_w_local():
        for i, w in enumerate(weights):
            pltpu.make_async_copy(wcols(w, c), wslot_one(i, d), wrecv.at[0, 0]).wait()

    def x_first(k):
        e = own[k]
        return (
            send(wslot(e), wslot(e), wsend.at[1, k], wrecv.at[1, k], xp),
            send(wslot(e), wslot(e), wsend.at[2, k], wrecv.at[2, k], xm),
        )

    def wpart(e, h):
        return wbuf.at[:, pl.ds(pl.multiple_of(e * WR + h * (WR // 2), WR // 2), WR // 2), :]

    def x_second(k):
        if k == 0:
            e = shift(own[0], 3)
            return send(wslot(e), wslot(e), wsend.at[3, k], wrecv.at[3, k], xp)
        if k == 1:
            e = shift(own[1], 1)
            return send(wslot(e), wslot(e), wsend.at[3, k], wrecv.at[3, k], xm)
        e = shift(own[2], 3 if k == 2 else 1)
        return send(wpart(e, k - 2), wpart(e, k - 2), wsend.at[3, k], wrecv.at[3, k], xp if k == 2 else xm)

    def y_second(k):
        to = chip_y((1, 3)[k % 2], c)
        if k < 2:
            e = shift(own[1], (3, 1)[k])
            return send(wslot(e), wslot(e), ysend.at[k], yrecv.at[k], to)
        e = shift(own[1], 2)
        return send(wpart(e, k - 2), wpart(e, k - 2), ysend.at[k], yrecv.at[k], to)

    def z_first(h):
        return (
            send(tslot(z, h), tslot(z, h), tsend.at[1, h], trecv.at[1, h], zp),
            send(tslot(z, h), tslot(z, h), tsend.at[2, h], trecv.at[2, h], zm),
        )

    def z_second(h):
        z_ = (z + (3, 1)[h // 2]) % 4
        return send(tslot(z_, h), tslot(z_, h), tsend.at[3, h], trecv.at[3, h], (zp, zm)[h // 2])

    zs = [z, (z + 3) % 4, (z + 1) % 4, (z + 2) % 4]

    def to_partner(g, h):
        return send(tslot(zs[g], h), tslot(zs[g], h), psend.at[g, h], precv.at[g, h], partner)

    def wait_t(g, h):
        send(tslot(zs[g], h), tslot(zs[g], h), tsend.at[1, h], trecv.at[g, h], partner).wait_recv()

    def wait_own_t(h):
        @pl.when(home)
        def _():
            pltpu.make_async_copy(tok.at[rows_of(h), :], tslot(z, h), trecv.at[0, h]).wait()

        @pl.when(away)
        def _():
            wait_t(0, h)

    def start_both(pair_):
        pair_[0].start()
        pair_[1].start()

    def x_start(k):
        if k == 0:
            wait_w_local()
        else:
            wait_w(0, k, own[k])
        start_both(x_first(k))

    def x_forward(k):
        wait_w(1 + k % 2, min(k, 2), shift(own[min(k, 2)], (3, 1)[k % 2]))
        x_second(k).start()

    def y_forward(k):
        if k == 0:
            wait_w(1, 1, shift(own[1], 3))
        if k == 2:
            wait_w(3, 1, shift(own[1], 2))
        y_second(k).start()

    def wait_y(k):
        there = wslot(shift(own[3], (3, 1)[k])) if k < 2 else wpart(shift(own[3], 2), k - 2)
        send(there, there, wsend.at[0, 0], yrecv.at[k], partner).wait_recv()

    def wait_nearby_w():
        wait_w(2, 0, shift(own[0], 1))
        wait_w(0, 3, own[3])
        wait_y(0)
        wait_y(1)

    def wait_across_w():
        wait_w(3, 0, shift(own[0], 2))
        for h in range(2):
            there = wpart(shift(own[2], 2), h)
            send(there, there, wsend.at[0, 0], wrecv.at[3, 2 + h], partner).wait_recv()
        wait_y(2)
        wait_y(3)

    def duty(role, g, h):
        @pl.when(role)
        def _():
            if g == 0:
                wait_own_t(h)
                z_first(h)[h // 2].start()
                if h == 3:
                    z_first(2)[0].start()
                    z_first(0)[1].start()
                    z_first(3)[0].start()
                    z_first(1)[1].start()
            else:
                wait_t(g, h)
                if (g, h // 2) in ((1, 0), (2, 1)):
                    z_second(h).start()
            to_partner(g, h).start()

    def ready(role, g, pieces=(0, 1, 2, 3)):
        @pl.when(role)
        def _():
            for h in pieces:
                there = tbuf.at[(1 - c) * 4 + zs[g], rows_of(h), :]
                send(there, there, psend.at[g, h], precv.at[g, h], partner).wait_recv()

    gain_row = gain[...].astype(jnp.float32).reshape(1, D)

    def norm(plane, g, pieces=(0, 3)):
        block = plane * 4 + zs[g]

        def norm_rows(i, carry):
            rows = tbuf[block, pl.ds(pl.multiple_of(i * NCHUNK, NCHUNK), NCHUNK), :].astype(jnp.float32)
            scale = lax.rsqrt(jnp.mean(rows * rows, axis=1, keepdims=True) + 1e-05)
            to = pl.ds(pl.multiple_of(block * ROWS + i * NCHUNK, NCHUNK), NCHUNK)
            nbuf[to, :] = (rows * scale * gain_row).astype(jnp.bfloat16)
            return carry

        lo, hi = PIECES[pieces[0]][0] // NCHUNK, sum(PIECES[pieces[1]]) // NCHUNK
        lax.fori_loop(lo, hi, norm_rows, 0, unroll=7)

    def turned(product, rows):
        cosine, sine = cosb[rows, :], sinb[rows, :]
        parts = []
        for h in range(2):
            v = product[:, h * HD : (h + 1) * HD]
            parts.append((v * cosine + pltpu.roll(v, HD // 2, 1) * sine).astype(jnp.bfloat16))
        return parts

    def dots(rows, i, chips):
        total = None
        for x_ in chips:
            depth = pl.ds(pl.multiple_of(x_ * 4 * WR, 4 * WR), 4 * WR)
            part = jnp.dot(nbuf[rows, depth], wbuf[i, depth, :], preferred_element_type=jnp.float32)
            total = part if total is None else total + part
        return total

    nearby, across = (x, (x + 3) % 4, (x + 1) % 4), (x + 2) % 4

    def project_nearby(first, local):
        rows = pl.ds(pl.multiple_of(first * ROWS, ROWS), 2 * ROWS)
        for i in range(3):
            lin[i, pl.ds(local * ROWS, 2 * ROWS), :] = dots(rows, i, nearby)

    def project(first, blocks, local=None):
        rows = pl.ds(pl.multiple_of(first * ROWS, ROWS), blocks * ROWS)

        def product(i):
            if local is None:
                return jnp.dot(nbuf[rows, :], wbuf[i], preferred_element_type=jnp.float32)
            return lin[i, pl.ds(local * ROWS, blocks * ROWS), :] + dots(rows, i, (across,))

        for buf, i in ((qbuf, 0), (kbuf, 1)):
            for h, part in enumerate(turned(product(i), rows)):
                buf[h, rows, :] = part
        v = product(2).astype(jnp.bfloat16)
        for h in range(2):
            vbuf[h, rows, :] = v[:, h * HD : (h + 1) * HD]

    def duties(role, g, pieces):
        for h in pieces:
            duty(role, g, h)

    x_start(0)
    duties(home, 0, (0, 2, 1, 3))
    x_start(1)
    ready(away, 0)
    norm(yh, 0)
    duty(home, 1, 0)
    duty(home, 2, 2)
    x_start(2)
    x_forward(0)
    duty(home, 1, 1)
    duty(home, 2, 3)
    x_forward(1)
    y_forward(0)
    y_forward(1)
    duty(away, 0, 0)
    duty(away, 0, 2)
    duties(home, 2, (0, 1))
    duties(home, 1, (2, 3))
    x_forward(2)
    x_forward(3)
    duties(away, 0, (1, 3))
    ready(away, 1)
    norm(yh, 1)
    ready(away, 2)
    norm(yh, 2)
    duty(away, 1, 0)
    duty(away, 2, 2)
    y_forward(2)
    y_forward(3)
    duties(home, 3, (0, 2, 1, 3))
    ready(home, 0)
    norm(1 - yh, 0)
    ready(away, 3)
    norm(yh, 3)
    duty(away, 1, 1)
    duty(away, 2, 3)
    wait_nearby_w()
    pltpu.make_async_copy(cos_hbm, cosb, lsem.at[0]).wait()
    pltpu.make_async_copy(sin_hbm, sinb, lsem.at[1]).wait()
    project_nearby(yh * 4, 0)
    project_nearby(yh * 4 + 2, 2)
    wait_across_w()
    project(yh * 4, 2, 0)
    duties(away, 1, (2, 3))
    duties(away, 2, (0, 1))
    project(yh * 4 + 2, 2, 2)
    ready(home, 1)
    norm(1 - yh, 1)
    ready(home, 2)
    norm(1 - yh, 2)
    project((1 - yh) * 4 + z - z % 2, 2)
    duty(away, 3, 0)
    duty(away, 3, 2)
    project((1 - yh) * 4 + (z + jnp.where(z % 2 == 0, 3, 1)) % 4, 1)
    duty(away, 3, 1)
    ready(home, 3, (0, 1))
    norm(1 - yh, 3, (0, 1))
    duty(away, 3, 3)
    ready(home, 3, (2, 3))
    norm(1 - yh, 3, (2, 3))
    project((1 - yh) * 4 + zs[3], 1)

    factor = HD ** (-0.5) * math.log2(math.e)
    nt = (((1,), (1,)), ((), ()))
    rows_i = lax.broadcasted_iota(jnp.int32, (QB, QB), 0)
    cols_i = lax.broadcasted_iota(jnp.int32, (QB, QB), 1)
    allowed = cols_i <= rows_i
    mycols = pl.ds(pl.multiple_of(z * 512 + c * WC, WC), WC)

    def parts(j):
        found = []
        for b in range(8):
            lo, hi = max(b * ROWS, j * QB), min((b + 1) * ROWS, (j + 1) * QB)
            if lo < hi:
                found.append((b, lo - b * ROWS, lo, hi - lo))
        return found

    def to_owner(b, first, row, n):
        return send(
            obuf.at[pl.ds(row, n), :], out.at[pl.ds(first, n), mycols], osend.at[b], orecv.at[z * 2 + c],
            dev(x, yl, yh, b // 4, b % 4),
        )

    def to_self(b, first, row, n):
        return pltpu.make_async_copy(obuf.at[pl.ds(row, n), :], out.at[pl.ds(first, n), mycols], osend.at[b])

    def own_block(b):
        return jnp.logical_and(home, t == b)

    def attend(b, h):
        rows, past = pl.ds(b * QB, QB), pl.ds(0, b * QB)
        q = qbuf[h, rows, :]
        s_d = lax.dot_general(q, kbuf[h, rows, :], nt, preferred_element_type=jnp.float32)
        s_d = jnp.where(allowed, s_d, -1e30)
        top = jnp.max(s_d, axis=1, keepdims=True)
        if b:
            s_p = lax.dot_general(q, kbuf[h, past, :], nt, preferred_element_type=jnp.float32)
            top = jnp.maximum(top, jnp.max(s_p, axis=1, keepdims=True))
        e_d = jnp.exp2((s_d - top) * factor)
        total = jnp.sum(e_d, axis=1, keepdims=True)
        acc = jnp.dot(e_d.astype(jnp.bfloat16), vbuf[h, rows, :], preferred_element_type=jnp.float32)
        if b:
            e_p = jnp.exp2((s_p - top) * factor)
            total = total + jnp.sum(e_p, axis=1, keepdims=True)
            acc = acc + jnp.dot(e_p.astype(jnp.bfloat16), vbuf[h, past, :], preferred_element_type=jnp.float32)
        obuf[rows, h * HD : (h + 1) * HD] = (acc / total).astype(jnp.bfloat16)

    def one_block(i, carry):
        first = (z + 1) % 4
        near = first - jnp.where(first > 1, 1, 0)
        early = jnp.where(i < 3, (near + i) % 3, 3 + (first + i - 3) % 4)
        late = jnp.where(i < 4, (first + i) % 4, 4 + (near + i - 4) % 3)
        j_ = jnp.where(yh == 0, early, late)
        for j in range(NQ):

            @pl.when(j_ == j)
            def _(j=j):
                for h in range(2):
                    attend(j, h)
                for part in parts(j):

                    @pl.when(own_block(part[0]))
                    def _(part=part):
                        to_self(*part).start()

                    @pl.when(jnp.logical_not(own_block(part[0])))
                    def _(part=part):
                        to_owner(*part).start()

        return carry

    lax.fori_loop(0, NQ, one_block, 0)

    for z_ in range(4):
        for c_ in range(2):
            cols = pl.ds((z_ * 2 + c_) * WC, WC)
            mine = jnp.logical_and(home, jnp.logical_and(z == z_, c == c_))

            @pl.when(jnp.logical_not(mine))
            def _(i=z_ * 2 + c_, cols=cols):
                send(obuf.at[pl.ds(0, ROWS), :], out.at[:, cols], osend.at[0], orecv.at[i], partner).wait_recv()

    for b in range(8):

        @pl.when(own_block(b))
        def _(b=b):
            to_self(b, 0, b * ROWS, ROWS).wait()

        @pl.when(jnp.logical_not(own_block(b)))
        def _(b=b):
            to_owner(b, 0, b * ROWS, ROWS).wait_send()

    for i in range(3):
        send(wslot(d), wslot(d), wsend.at[0, i], wrecv.at[0, 0], partner).wait_send()
    for k in range(4):
        if k < 3:
            for copy in x_first(k):
                copy.wait_send()
        x_second(k).wait_send()
        y_second(k).wait_send()
    for h in range(4):

        @pl.when(away)
        def _(h=h):
            exchange(h).wait_send()

        for copy in z_first(h):
            copy.wait_send()
        z_second(h).wait_send()
        for g in range(4):
            to_partner(g, h).wait_send()


def shards(tokens, norm_gain, q_weight, k_weight, v_weight):
    cosine, sine = tables()
    anywhere = pl.BlockSpec(memory_space=pl.ANY)
    bf, dma = jnp.bfloat16, pltpu.SemaphoreType.DMA
    attended = pl.pallas_call(
        kernel,
        out_shape=jax.ShapeDtypeStruct((ROWS, D), bf),
        in_specs=[anywhere, pl.BlockSpec(memory_space=pltpu.VMEM)] + [anywhere] * 5,
        out_specs=anywhere,
        scratch_shapes=[
            pltpu.VMEM((8, ROWS, D), bf),
            pltpu.VMEM((LEN, D), bf),
            pltpu.VMEM((3, D, WC), bf),
            pltpu.VMEM((3, 4 * ROWS, WC), jnp.float32),
            pltpu.VMEM((2, LEN, HD), bf),
            pltpu.VMEM((2, LEN, HD), bf),
            pltpu.VMEM((2, LEN, HD), bf),
            pltpu.VMEM((LEN, WC), bf),
            pltpu.VMEM((LEN, HD), jnp.float32),
            pltpu.VMEM((LEN, HD), jnp.float32),
            dma((4,)),
            dma((4,)),
            dma((4, 4)),
            dma((4, 4)),
            dma((4, 4)),
            dma((4, 4)),
            dma((4, 4)),
            dma((4, 4)),
            dma((8,)),
            dma((8,)),
            dma((2,)),
        ],
        compiler_params=pltpu.CompilerParams(
            collective_id=0, has_side_effects=True, vmem_limit_bytes=60 * 2**20
        ),
        name="attention_block",
    )(tokens[0], norm_gain, q_weight, k_weight, v_weight, jnp.asarray(cosine), jnp.asarray(sine))
    return attended[None]


def solution(mesh):
    placed = (P("dp", "ctx", None), P(), P("dp", None), P("dp", None), P("dp", None))
    return jax.shard_map(
        shards, mesh=mesh, in_specs=placed, out_specs=P("dp", "ctx", None), check_vma=False
    )
```

```python
import functools
import math

import jax
import jax.numpy as jnp
import numpy as np
from jax import lax
from jax.experimental import pallas as pl
from jax.experimental.pallas import tpu as pltpu
from jax.sharding import PartitionSpec as P

MESH = pl.DeviceIdType.MESH
HEADS = 16
HD = 128
D = 2048
ROWS = 224
LEN = 1792
WR = 128
WC = 256
QB = 256
NQ = LEN // QB
PIECES = ((0, 64), (64, 48), (112, 64), (176, 48))
NCHUNK = 16


def tables():
    freqs = 10000.0 ** (-2.0 * np.arange(HD // 2) / HD)
    angles = np.arange(LEN)[:, None] * freqs[None, :]
    cosine, sine = np.cos(angles), np.sin(angles)
    return (
        np.concatenate([cosine, cosine], axis=1).astype(np.float32),
        np.concatenate([-sine, sine], axis=1).astype(np.float32),
    )


def kernel(
    tok, gain, qw, kw, vw, cos_hbm, sin_hbm, out,
    tbuf, nbuf, wbuf, lin, qbuf, kbuf, vbuf, obuf, cosb, sinb,
    yrecv, ysend, wrecv, wsend, trecv, tsend, precv, psend, osend, orecv, lsem,
):
    d, t = lax.axis_index("dp"), lax.axis_index("ctx")
    x, yl, c = d // 4, (d // 2) % 2, d % 2
    yh, z = t // 4, t % 4
    y = yh * 2 + yl
    home = c == yh
    away = c != yh

    def dev(x_, yl_, c_, yh_, z_):
        return (x_ * 4 + yl_ * 2 + c_, yh_ * 4 + z_)

    def chip_y(step, c_):
        y_ = (y + step) % 4
        return dev(x, y_ % 2, c_, y_ // 2, z)

    partner = dev(x, yl, 1 - c, yh, z)
    pair = dev(x, yl, 1 - c, 1 - yh, z)
    xp, xm = dev((x + 1) % 4, yl, c, yh, z), dev((x + 3) % 4, yl, c, yh, z)
    zp, zm = dev(x, yl, c, yh, (z + 1) % 4), dev(x, yl, c, yh, (z + 3) % 4)

    def send(src, dst, ss, rs, to):
        return pltpu.make_async_remote_copy(
            src_ref=src, dst_ref=dst, send_sem=ss, recv_sem=rs, device_id=to, device_id_type=MESH
        )

    def wslot(e):
        return wbuf.at[:, pl.ds(pl.multiple_of(e * WR, WR), WR), :]

    def wslot_one(i, e):
        return wbuf.at[i, pl.ds(pl.multiple_of(e * WR, WR), WR), :]

    def wcols(ref, c_):
        return ref.at[:, pl.ds(pl.multiple_of(z * 512 + c_ * WC, WC), WC)]

    def rows_of(i):
        return pl.ds(*PIECES[i])

    def tslot(z_, h):
        return tbuf.at[c * 4 + z_, rows_of(h), :]

    weights = (qw, kw, vw)
    for i, w in enumerate(weights):
        pltpu.make_async_copy(wcols(w, c), wslot_one(i, d), wrecv.at[0, 0]).start()

    @pl.when(home)
    def _():
        for h in range(4):
            pltpu.make_async_copy(tok.at[rows_of(h), :], tslot(z, h), trecv.at[0, h]).start()

    pltpu.make_async_copy(cos_hbm, cosb, lsem.at[0]).start()
    pltpu.make_async_copy(sin_hbm, sinb, lsem.at[1]).start()

    barrier = pltpu.get_barrier_semaphore()

    def greet(to):
        pl.semaphore_signal(barrier, inc=1, device_id=to, device_id_type=MESH)

    for to in (partner, pair, xp, xm, zp, zm):
        greet(to)
    for step in (1, 3):
        for c_ in range(2):
            greet(chip_y(step, c_))
    pl.semaphore_wait(barrier, 10)

    for i, w in enumerate(weights):
        send(wcols(w, c), wslot_one(i, d), wsend.at[0, 0], wrecv.at[0, 2], chip_y(1, c)).start()
        send(wcols(w, 1 - c), wslot_one(i, d), wsend.at[0, 2], wrecv.at[0, 1], partner).start()

    def exchange(h):
        there = tbuf.at[(1 - c) * 4 + z, rows_of(h), :]
        return send(tok.at[rows_of(h), :], there, tsend.at[0, h], trecv.at[0, h], pair)

    @pl.when(away)
    def _():
        for h in (0, 2, 1, 3):
            exchange(h).start()

    for i, w in enumerate(weights):
        send(wcols(w, 1 - c), wslot_one(i, d), wsend.at[0, 1], wrecv.at[0, 3], chip_y(3, 1 - c)).start()

    own = [d, x * 4 + yl * 2 + (1 - c), x * 4 + (1 - yl) * 2 + c, x * 4 + (1 - yl) * 2 + (1 - c)]

    def shift(e, s):
        return (e + 4 * s) % 16

    def wait_w(g, k, e):
        send(wslot(e), wslot(e), wsend.at[0, 0], wrecv.at[g, k], partner).wait_recv()

    def wait_w_local():
        for i, w in enumerate(weights):
            pltpu.make_async_copy(wcols(w, c), wslot_one(i, d), wrecv.at[0, 0]).wait()

    def x_first(k):
        e = own[k]
        return (
            send(wslot(e), wslot(e), wsend.at[1, k], wrecv.at[1, k], xp),
            send(wslot(e), wslot(e), wsend.at[2, k], wrecv.at[2, k], xm),
        )

    def wpart(e, h):
        return wbuf.at[:, pl.ds(pl.multiple_of(e * WR + h * (WR // 2), WR // 2), WR // 2), :]

    def x_second(k):
        if k == 0:
            e = shift(own[0], 3)
            return send(wslot(e), wslot(e), wsend.at[3, k], wrecv.at[3, k], xp)
        if k == 1:
            e = shift(own[1], 1)
            return send(wslot(e), wslot(e), wsend.at[3, k], wrecv.at[3, k], xm)
        e = shift(own[2], 3 if k == 2 else 1)
        return send(wpart(e, k - 2), wpart(e, k - 2), wsend.at[3, k], wrecv.at[3, k], xp if k == 2 else xm)

    def y_second(k):
        to = chip_y((1, 3)[k % 2], c)
        if k < 2:
            e = shift(own[1], (3, 1)[k])
            return send(wslot(e), wslot(e), ysend.at[k], yrecv.at[k], to)
        e = shift(own[1], 2)
        return send(wpart(e, k - 2), wpart(e, k - 2), ysend.at[k], yrecv.at[k], to)

    def z_first(h):
        return (
            send(tslot(z, h), tslot(z, h), tsend.at[1, h], trecv.at[1, h], zp),
            send(tslot(z, h), tslot(z, h), tsend.at[2, h], trecv.at[2, h], zm),
        )

    def z_second(h):
        z_ = (z + (3, 1)[h // 2]) % 4
        return send(tslot(z_, h), tslot(z_, h), tsend.at[3, h], trecv.at[3, h], (zp, zm)[h // 2])

    zs = [z, (z + 3) % 4, (z + 1) % 4, (z + 2) % 4]

    def to_partner(g, h):
        return send(tslot(zs[g], h), tslot(zs[g], h), psend.at[g, h], precv.at[g, h], partner)

    def wait_t(g, h):
        send(tslot(zs[g], h), tslot(zs[g], h), tsend.at[1, h], trecv.at[g, h], partner).wait_recv()

    def wait_own_t(h):
        @pl.when(home)
        def _():
            pltpu.make_async_copy(tok.at[rows_of(h), :], tslot(z, h), trecv.at[0, h]).wait()

        @pl.when(away)
        def _():
            wait_t(0, h)

    def start_both(pair_):
        pair_[0].start()
        pair_[1].start()

    def x_start(k):
        if k == 0:
            wait_w_local()
        else:
            wait_w(0, k, own[k])
        start_both(x_first(k))

    def x_forward(k):
        wait_w(1 + k % 2, min(k, 2), shift(own[min(k, 2)], (3, 1)[k % 2]))
        x_second(k).start()

    def y_forward(k):
        if k == 0:
            wait_w(1, 1, shift(own[1], 3))
        if k == 2:
            wait_w(3, 1, shift(own[1], 2))
        y_second(k).start()

    def wait_y(k):
        there = wslot(shift(own[3], (3, 1)[k])) if k < 2 else wpart(shift(own[3], 2), k - 2)
        send(there, there, wsend.at[0, 0], yrecv.at[k], partner).wait_recv()

    def wait_nearby_w():
        wait_w(2, 0, shift(own[0], 1))
        wait_w(0, 3, own[3])
        wait_y(0)
        wait_y(1)

    def wait_across_w():
        wait_w(3, 0, shift(own[0], 2))
        for h in range(2):
            there = wpart(shift(own[2], 2), h)
            send(there, there, wsend.at[0, 0], wrecv.at[3, 2 + h], partner).wait_recv()
        wait_y(2)
        wait_y(3)

    def duty(role, g, h):
        @pl.when(role)
        def _():
            if g == 0:
                wait_own_t(h)
                z_first(h)[h // 2].start()
                if h == 3:
                    z_first(2)[0].start()
                    z_first(0)[1].start()
                    z_first(3)[0].start()
                    z_first(1)[1].start()
            else:
                wait_t(g, h)
                if (g, h // 2) in ((1, 0), (2, 1)):
                    z_second(h).start()
            to_partner(g, h).start()

    def ready(role, g, pieces=(0, 1, 2, 3)):
        @pl.when(role)
        def _():
            for h in pieces:
                there = tbuf.at[(1 - c) * 4 + zs[g], rows_of(h), :]
                send(there, there, psend.at[g, h], precv.at[g, h], partner).wait_recv()

    gain_row = gain[...].astype(jnp.float32).reshape(1, D)

    def norm(plane, g, pieces=(0, 3)):
        block = plane * 4 + zs[g]

        def norm_rows(i, carry):
            rows = tbuf[block, pl.ds(pl.multiple_of(i * NCHUNK, NCHUNK), NCHUNK), :].astype(jnp.float32)
            scale = lax.rsqrt(jnp.mean(rows * rows, axis=1, keepdims=True) + 1e-05)
            to = pl.ds(pl.multiple_of(block * ROWS + i * NCHUNK, NCHUNK), NCHUNK)
            nbuf[to, :] = (rows * scale * gain_row).astype(jnp.bfloat16)
            return carry

        lo, hi = PIECES[pieces[0]][0] // NCHUNK, sum(PIECES[pieces[1]]) // NCHUNK
        lax.fori_loop(lo, hi, norm_rows, 0, unroll=7)

    def turned(product, rows):
        cosine, sine = cosb[rows, :], sinb[rows, :]
        parts = []
        for h in range(2):
            v = product[:, h * HD : (h + 1) * HD]
            parts.append((v * cosine + pltpu.roll(v, HD // 2, 1) * sine).astype(jnp.bfloat16))
        return parts

    def dots(rows, i, chips):
        total = None
        for x_ in chips:
            depth = pl.ds(pl.multiple_of(x_ * 4 * WR, 4 * WR), 4 * WR)
            part = jnp.dot(nbuf[rows, depth], wbuf[i, depth, :], preferred_element_type=jnp.float32)
            total = part if total is None else total + part
        return total

    nearby, across = (x, (x + 3) % 4, (x + 1) % 4), (x + 2) % 4

    def project_nearby(first, local):
        rows = pl.ds(pl.multiple_of(first * ROWS, ROWS), 2 * ROWS)
        for i in range(3):
            lin[i, pl.ds(local * ROWS, 2 * ROWS), :] = dots(rows, i, nearby)

    def project(first, blocks, local=None):
        rows = pl.ds(pl.multiple_of(first * ROWS, ROWS), blocks * ROWS)

        def product(i):
            if local is None:
                return jnp.dot(nbuf[rows, :], wbuf[i], preferred_element_type=jnp.float32)
            return lin[i, pl.ds(local * ROWS, blocks * ROWS), :] + dots(rows, i, (across,))

        for buf, i in ((qbuf, 0), (kbuf, 1)):
            for h, part in enumerate(turned(product(i), rows)):
                buf[h, rows, :] = part
        v = product(2).astype(jnp.bfloat16)
        for h in range(2):
            vbuf[h, rows, :] = v[:, h * HD : (h + 1) * HD]

    def duties(role, g, pieces):
        for h in pieces:
            duty(role, g, h)

    x_start(0)
    duties(home, 0, (0, 2, 1, 3))
    x_start(1)
    ready(away, 0)
    norm(yh, 0)
    duty(home, 1, 0)
    duty(home, 2, 2)
    x_start(2)
    x_forward(0)
    duty(home, 1, 1)
    duty(home, 2, 3)
    x_forward(1)
    y_forward(0)
    y_forward(1)
    duty(away, 0, 0)
    duty(away, 0, 2)
    duties(home, 2, (0, 1))
    duties(home, 1, (2, 3))
    x_forward(2)
    x_forward(3)
    duties(away, 0, (1, 3))
    ready(away, 1)
    norm(yh, 1)
    ready(away, 2)
    norm(yh, 2)
    duty(away, 1, 0)
    duty(away, 2, 2)
    y_forward(2)
    y_forward(3)
    duties(home, 3, (0, 2, 1, 3))
    ready(home, 0)
    norm(1 - yh, 0)
    ready(away, 3)
    norm(yh, 3)
    duty(away, 1, 1)
    duty(away, 2, 3)
    wait_nearby_w()
    pltpu.make_async_copy(cos_hbm, cosb, lsem.at[0]).wait()
    pltpu.make_async_copy(sin_hbm, sinb, lsem.at[1]).wait()
    project_nearby(yh * 4, 0)
    project_nearby(yh * 4 + 2, 2)
    wait_across_w()
    project(yh * 4, 2, 0)
    duties(away, 1, (2, 3))
    duties(away, 2, (0, 1))
    project(yh * 4 + 2, 2, 2)
    ready(home, 1)
    norm(1 - yh, 1)
    ready(home, 2)
    norm(1 - yh, 2)
    project((1 - yh) * 4 + z - z % 2, 2)
    duty(away, 3, 0)
    duty(away, 3, 2)
    project((1 - yh) * 4 + (z + jnp.where(z % 2 == 0, 3, 1)) % 4, 1)
    duty(away, 3, 1)
    ready(home, 3, (0, 1))
    norm(1 - yh, 3, (0, 1))
    duty(away, 3, 3)
    ready(home, 3, (2, 3))
    norm(1 - yh, 3, (2, 3))
    project((1 - yh) * 4 + zs[3], 1)

    factor = HD ** (-0.5) * math.log2(math.e)
    nt = (((1,), (1,)), ((), ()))
    rows_i = lax.broadcasted_iota(jnp.int32, (QB, QB), 0)
    cols_i = lax.broadcasted_iota(jnp.int32, (QB, QB), 1)
    allowed = cols_i <= rows_i
    mycols = pl.ds(pl.multiple_of(z * 512 + c * WC, WC), WC)

    def parts(j):
        found = []
        for b in range(8):
            lo, hi = max(b * ROWS, j * QB), min((b + 1) * ROWS, (j + 1) * QB)
            if lo < hi:
                found.append((b, lo - b * ROWS, lo, hi - lo))
        return found

    def to_owner(b, first, row, n):
        return send(
            obuf.at[pl.ds(row, n), :], out.at[pl.ds(first, n), mycols], osend.at[b], orecv.at[z * 2 + c],
            dev(x, yl, yh, b // 4, b % 4),
        )

    def to_self(b, first, row, n):
        return pltpu.make_async_copy(obuf.at[pl.ds(row, n), :], out.at[pl.ds(first, n), mycols], osend.at[b])

    def own_block(b):
        return jnp.logical_and(home, t == b)

    def attend(b):
        rows, past = pl.ds(b * QB, QB), pl.ds(0, b * QB)
        both, spans = range(2), (rows, past) if b else (rows,)
        scores = [
            [
                lax.dot_general(qbuf[h, rows, :], kbuf[h, span, :], nt, preferred_element_type=jnp.float32)
                for span in spans
            ]
            for h in both
        ]
        for h in both:
            scores[h][0] = jnp.where(allowed, scores[h][0], -1e30)
        top = [functools.reduce(jnp.maximum, [jnp.max(p, axis=1, keepdims=True) for p in scores[h]]) for h in both]
        expo = [[jnp.exp2((p - top[h]) * factor) for p in scores[h]] for h in both]
        total = [sum(jnp.sum(p, axis=1, keepdims=True) for p in expo[h]) for h in both]
        for h in both:
            acc = sum(
                jnp.dot(p.astype(jnp.bfloat16), vbuf[h, span, :], preferred_element_type=jnp.float32)
                for p, span in zip(expo[h], spans)
            )
            obuf[rows, h * HD : (h + 1) * HD] = (acc / total[h]).astype(jnp.bfloat16)

    def one_block(i, carry):
        first = (z + 1) % 4
        near = first - jnp.where(first > 1, 1, 0)
        early = jnp.where(i < 3, (near + i) % 3, 3 + (first + i - 3) % 4)
        late = jnp.where(i < 4, (first + i) % 4, 4 + (near + i - 4) % 3)
        j_ = jnp.where(yh == 0, early, late)
        for j in range(NQ):

            @pl.when(j_ == j)
            def _(j=j):
                attend(j)
                for part in parts(j):

                    @pl.when(own_block(part[0]))
                    def _(part=part):
                        to_self(*part).start()

                    @pl.when(jnp.logical_not(own_block(part[0])))
                    def _(part=part):
                        to_owner(*part).start()

        return carry

    lax.fori_loop(0, NQ, one_block, 0)

    for z_ in range(4):
        for c_ in range(2):
            cols = pl.ds((z_ * 2 + c_) * WC, WC)
            mine = jnp.logical_and(home, jnp.logical_and(z == z_, c == c_))

            @pl.when(jnp.logical_not(mine))
            def _(i=z_ * 2 + c_, cols=cols):
                send(obuf.at[pl.ds(0, ROWS), :], out.at[:, cols], osend.at[0], orecv.at[i], partner).wait_recv()

    for b in range(8):

        @pl.when(own_block(b))
        def _(b=b):
            to_self(b, 0, b * ROWS, ROWS).wait()

        @pl.when(jnp.logical_not(own_block(b)))
        def _(b=b):
            to_owner(b, 0, b * ROWS, ROWS).wait_send()

    for i in range(3):
        send(wslot(d), wslot(d), wsend.at[0, i], wrecv.at[0, 0], partner).wait_send()
    for k in range(4):
        if k < 3:
            for copy in x_first(k):
                copy.wait_send()
        x_second(k).wait_send()
        y_second(k).wait_send()
    for h in range(4):

        @pl.when(away)
        def _(h=h):
            exchange(h).wait_send()

        for copy in z_first(h):
            copy.wait_send()
        z_second(h).wait_send()
        for g in range(4):
            to_partner(g, h).wait_send()


def shards(tokens, norm_gain, q_weight, k_weight, v_weight):
    cosine, sine = tables()
    anywhere = pl.BlockSpec(memory_space=pl.ANY)
    bf, dma = jnp.bfloat16, pltpu.SemaphoreType.DMA
    attended = pl.pallas_call(
        kernel,
        out_shape=jax.ShapeDtypeStruct((ROWS, D), bf),
        in_specs=[anywhere, pl.BlockSpec(memory_space=pltpu.VMEM)] + [anywhere] * 5,
        out_specs=anywhere,
        scratch_shapes=[
            pltpu.VMEM((8, ROWS, D), bf),
            pltpu.VMEM((LEN, D), bf),
            pltpu.VMEM((3, D, WC), bf),
            pltpu.VMEM((3, 4 * ROWS, WC), jnp.float32),
            pltpu.VMEM((2, LEN, HD), bf),
            pltpu.VMEM((2, LEN, HD), bf),
            pltpu.VMEM((2, LEN, HD), bf),
            pltpu.VMEM((LEN, WC), bf),
            pltpu.VMEM((LEN, HD), jnp.float32),
            pltpu.VMEM((LEN, HD), jnp.float32),
            dma((4,)),
            dma((4,)),
            dma((4, 4)),
            dma((4, 4)),
            dma((4, 4)),
            dma((4, 4)),
            dma((4, 4)),
            dma((4, 4)),
            dma((8,)),
            dma((8,)),
            dma((2,)),
        ],
        compiler_params=pltpu.CompilerParams(
            collective_id=0, has_side_effects=True, vmem_limit_bytes=60 * 2**20
        ),
        name="attention_block",
    )(tokens[0], norm_gain, q_weight, k_weight, v_weight, jnp.asarray(cosine), jnp.asarray(sine))
    return attended[None]


def solution(mesh):
    placed = (P("dp", "ctx", None), P(), P("dp", None), P("dp", None), P("dp", None))
    return jax.shard_map(
        shards, mesh=mesh, in_specs=placed, out_specs=P("dp", "ctx", None), check_vma=False
    )
```
